32 devices in a mesh: tm: 4 (over y, x), games: 4 (over z), member: 2 (over core).
Axes of the slice: x: 2, y: 2, z: 4, core: 2. Of those that a mesh axis runs over, the one named last changes fastest.
Arguments:
- rewards: float32 [32, 16384], P('games', 'tm'), as said below
- dones: int32 [32, 16384], P('games', 'tm'), may hold values 0 or 1
- values: float32 [2, 32, 16384], P('member', 'games', 'tm'), may hold values from -6 to 6
- discount: float32 [32], P('games'), as said below
- trace: float32 [32], P('games'), as said below
Outputs:
- returns: float32 [32, 16384], P('games', 'tm')
- advantages: float32 [32, 16384], P('games', 'tm')
- value_loss: float32 [2, 32], P('member', 'games')
The draws below stay inside these ranges and needn't reach their ends.
Inputs may be any that keep to these rules, and one draw needn't show every extreme that they name: rewards lie between -3.6 and 3.6. Each discount lies between 1 - 1/30 and 1 - 1/1048576. Each trace lies between 1 - 1/30 and 1 - 1/1048576.
All inputs are finite; a program needn't handle non-finite values. No bound on the sum of `dones` on one device may be relied on, other than what follows from the above.
Results may differ from the reference program's by a relative error of at most 0.0003.
Values sent between devices are 32-bit elements; how exact they have to be, the bound alone decides.
No kernel may reach another device: no remote copies, remote signals or barrier semaphores. Data moves between devices by JAX's collectives and lax.ppermute only.
A program may use at most 64 MiB of HBM per device.

```python
import math
import jax
import jax.numpy as jnp
from jax import lax

GAMES = 32
MOVES = 16384
MEMBERS = 2


def spread_scales(key, count, spread):
    return jnp.exp(jax.random.uniform(key, (count,), jnp.float32, 0.0, math.log(spread)))


def horizon(key, lowest, highest):
    return jnp.exp(jax.random.uniform(key, (GAMES,), jnp.float32, math.log(lowest), math.log(highest)))


def draw_rewards(key, part):
    row_scale = spread_scales(jax.random.fold_in(key, 1), GAMES, 10.0)
    col_scale = spread_scales(jax.random.fold_in(key, 2), MOVES, 10.0)
    rising = 1.0 + 2.0 * jnp.arange(GAMES, dtype=jnp.float32) / GAMES
    along = 1.0 + 2.0 * jnp.arange(MOVES, dtype=jnp.float32) / MOVES
    core = jax.random.truncated_normal(jax.random.fold_in(key, 3), -4.0, 4.0, (GAMES, MOVES), jnp.float32)
    return 0.001 * core * (row_scale * rising)[:, None] * (col_scale * along)[None, :]


def draw_discount(key, part):
    length = horizon(jax.random.fold_in(key, 5), 30.0, 64.0 * MOVES)
    return 1.0 - 1.0 / length


def draw_trace(key, part):
    length = horizon(jax.random.fold_in(key, 6), 30.0, 64.0 * MOVES)
    return 1.0 - 1.0 / length


def set_ends(entries, stream_key, least, high):
    longest = entries.shape.index(max(entries.shape))
    spots = []
    for shift in (0, 1):
        where = [jax.random.randint(jax.random.fold_in(stream_key, axis), (), 0, length) for axis, length in enumerate(entries.shape)]
        where[longest] = (where[longest] + shift) % entries.shape[longest]
        spots.append(tuple(where))
    return entries.at[spots[0]].set(least).at[spots[1]].set(high)


def block_levels(own_key, extent, cuts, least, top_value):
    factor_of, own = 1.0, jax.random.fold_in(own_key, 6)
    for dim, shards_of in cuts:
        steps = jnp.exp(jax.random.uniform(jax.random.fold_in(own, dim), (shards_of,), jnp.float32, least / len(cuts), top_value / len(cuts)))
        factor_of = factor_of * jnp.repeat(steps, extent[dim] // shards_of).reshape([-1 if axis == dim else 1 for axis in range(len(extent))])
    return factor_of


def scatter_about(own_key, extent, width, most, split=(), held_as=jnp.bfloat16):
    drawn = width * jax.random.normal(own_key, extent, jnp.float32)
    if split:
        drawn = drawn * block_levels(own_key, extent, split, -0.22, 0.18)
    return jnp.clip(drawn, -most, most).astype(held_as)


def setup_inputs(seed: int = 0) -> dict:
    splits = jax.random.split(jax.random.key(seed), 6)
    rewards = draw_rewards(jax.random.fold_in(splits[5], 71), 0)
    dones = set_ends((jax.random.randint(splits[1], (GAMES, MOVES), 0, 4 * MOVES) < 1).astype(jnp.int32), jax.random.fold_in(splits[1], 1), 0, 1)
    values = scatter_about(splits[2], (MEMBERS, GAMES, MOVES), 1.0, 6.0, ((0, 2), (1, 4), (2, 4)), jnp.float32)
    discount = draw_discount(jax.random.fold_in(splits[5], 71), 0)
    trace = draw_trace(jax.random.fold_in(splits[5], 71), 0)
    return {"rewards": rewards, "dones": dones, "values": values, "discount": discount, "trace": trace}


def reference(rewards, dones, values, discount, trace):
    mean_value = lax.optimization_barrier(jnp.sum(values, axis=0)) / MEMBERS
    next_value = jnp.concatenate([mean_value[:, 1:], jnp.zeros((GAMES, 1), jnp.float32)], axis=1)
    keep_mask = 1.0 - dones.astype(jnp.float32)
    decay_rate = discount[:, None] * trace[:, None] * keep_mask
    offset = rewards + discount[:, None] * keep_mask * (1.0 - trace[:, None]) * next_value

    def back_step(carry_in, inputs):
        result = inputs[0] * carry_in + inputs[1]
        return (result, result)
    _, stacked = lax.scan(back_step, jnp.zeros((GAMES,), jnp.float32), (decay_rate.T, offset.T), reverse=True)
    returns = stacked.T
    raw_adv = returns - mean_value
    norm_scale = lax.rsqrt(jnp.mean(raw_adv * raw_adv) + 1e-06)
    advantages = raw_adv * norm_scale
    error_term = values - returns[None]
    value_loss = lax.optimization_barrier(jnp.mean(error_term * error_term, axis=2))
    return (returns, advantages, value_loss)
```

```python
import functools

import jax
import jax.numpy as jnp
from jax import lax
from jax.experimental import pallas as pl
from jax.experimental.pallas import tpu as pltpu
from jax.sharding import PartitionSpec as P

LANES = 128
SLOT = 16
GROUPS = LANES // SLOT
VMEM = pl.BlockSpec(memory_space=pltpu.VMEM)


def iotas(rows):
    shape = (rows, LANES)
    return (
        lax.broadcasted_iota(jnp.int32, shape, 0),
        lax.broadcasted_iota(jnp.int32, shape, 1),
    )


def spread(column, rows):
    return jnp.broadcast_to(column, (rows, LANES))


def to_column(row, rows):
    sub, lane = iotas(rows)
    padded = jnp.broadcast_to(jnp.pad(row, ((0, 0), (0, LANES - rows))), (rows, LANES))
    return spread(jnp.sum(jnp.where(lane == sub, padded, 0.0), axis=1, keepdims=True), rows)


def local_kernel(
    members, rewards, dones, own, other, discount, trace, scan_out, alpha_out, mean_out, stats_out
):
    rows, moves = rewards.shape
    tiles = moves // LANES
    sub, lane = iotas(rows)
    last_block = lax.axis_index("tm") == lax.axis_size("tm") - 1
    offset_lane = lax.rem(lax.axis_index("games"), GROUPS) * SLOT

    disc = to_column(discount[...], rows)
    lam = to_column(trace[...], rows)
    rate = disc * lam
    boot = disc * (1.0 - lam)

    def tile(ref, j):
        return ref[:, j * LANES : (j + 1) * LANES]

    own_last = own[:, moves - 1 : moves]
    mean_last = (own_last + other[:, moves - 1 : moves]) / members
    reward_last = rewards[:, moves - 1 : moves]
    guess = jnp.where(last_block, 0.0, spread(mean_last - reward_last, rows) / rate)
    own_guess = jnp.where(last_block, 0.0, spread(own_last - reward_last, rows) / rate)
    gap = own_guess - guess

    carry, scale = guess, jnp.ones((rows, LANES), jnp.float32)
    ahead = jnp.zeros((rows, LANES), jnp.float32)
    zero = jnp.zeros((rows, LANES), jnp.float32)
    suu, sua, saa, sqq, sqa = zero, zero, zero, zero, zero
    for j in reversed(range(tiles)):
        mine = tile(own, j)
        mean = (mine + tile(other, j)) / members
        mean_out[:, j * LANES : (j + 1) * LANES] = mean
        shifted = pltpu.roll(mean, LANES - 1, 1)
        following = jnp.where(lane == LANES - 1, ahead, shifted)
        ahead = shifted
        keep = 1.0 - tile(dones, j).astype(jnp.float32)
        a = rate * keep
        b = tile(rewards, j) + boot * keep * following
        step = 1
        while step < LANES:
            inside = lane < LANES - step
            b = b + jnp.where(inside, a, 0.0) * pltpu.roll(b, LANES - step, 1)
            a = jnp.where(inside, a * pltpu.roll(a, LANES - step, 1), a)
            step *= 2
        result = b + a * carry
        alpha = a * scale
        scan_out[:, j * LANES : (j + 1) * LANES] = result
        alpha_out[:, j * LANES : (j + 1) * LANES] = alpha
        a_head, b_head = spread(a[:, :1], rows), spread(b[:, :1], rows)
        carry = b_head + a_head * carry
        scale = a_head * scale
        u = result - mean
        q = mine - result - alpha * gap
        suu += u * u
        sua += u * alpha
        saa += alpha * alpha
        sqq += q * q
        sqa += q * alpha

    def total(x):
        return spread(jnp.sum(x, axis=1, keepdims=True), rows)

    mean_head = spread(mean_out[:, :1], rows)
    entries = (
        carry + (1.0 - lam) / lam * mean_head,
        scale,
        guess,
        total(suu),
        total(sua),
        total(saa),
        own_guess,
        total(sqq),
        total(sqa),
    )
    stats = zero
    for k, entry in enumerate(entries):
        stats = jnp.where(lane == offset_lane + k, entry, stats)
    stats_out[...] = jnp.broadcast_to(stats[None], stats_out.shape)


def final_kernel(
    blocks, groups, moves_all, cells_all, scan, alpha, mean, stats, returns_out, adv_out, loss_out
):
    rows, moves = scan.shape
    tiles = moves // LANES
    sub, lane = iotas(rows)
    block = lax.axis_index("tm")
    group = lax.axis_index("games")
    slot = lax.rem(group, GROUPS) * SLOT

    squares = jnp.zeros((rows, LANES), jnp.float32)
    own_eps = jnp.zeros((rows, LANES), jnp.float32)
    own_loss = jnp.zeros((rows, LANES), jnp.float32)
    for first in range(0, groups, GROUPS):
        last = min(first + GROUPS, groups)
        here = (lane == slot) & (group >= first) & (group < last)
        valid = (lax.rem(lane, SLOT) == 0) & (lane < (last - first) * SLOT)
        ahead = jnp.zeros((rows, LANES), jnp.float32)
        for t in reversed(range(blocks)):
            merged = stats[t * groups + first]
            for g in range(first + 1, last):
                merged = merged + stats[t * groups + g]
            pick = [merged] + [pltpu.roll(merged, LANES - k, 1) for k in range(1, 9)]
            head, slope, guess, suu, sua, saa, own_guess, sqq, sqa = pick
            eps = ahead - guess
            own = ahead - own_guess
            ahead = head + slope * eps
            squares += jnp.where(valid, suu + eps * (2.0 * sua + eps * saa), 0.0)
            own_loss += jnp.where(here, sqq + own * (own * saa - 2.0 * sqa), 0.0)
            own_eps += jnp.where(here & (block == t), eps, 0.0)

    eps = spread(jnp.sum(own_eps, axis=1, keepdims=True), rows)
    total = jnp.sum(jnp.sum(squares, axis=1, keepdims=True), axis=0, keepdims=True)
    norm_scale = jnp.broadcast_to(lax.rsqrt(total / cells_all + 1e-06), (rows, LANES))
    loss = spread(jnp.sum(own_loss, axis=1, keepdims=True), rows)
    loss_row = jnp.sum(jnp.where(lane == sub, loss, 0.0), axis=0, keepdims=True)
    loss_out[...] = loss_row[:, :rows] / moves_all
    for j in range(tiles):
        at = slice(j * LANES, (j + 1) * LANES)
        result = scan[:, at] + alpha[:, at] * eps
        returns_out[:, at] = result
        adv_out[:, at] = (result - mean[:, at]) * norm_scale


def per_device(rewards, dones, values, discount, trace):
    members = lax.axis_size("member")
    blocks = lax.axis_size("tm")
    groups = lax.axis_size("games")
    own = values[0]
    rows, moves = own.shape
    other = None
    for turn in range(1, members):
        got = lax.ppermute(own, "member", [(m, (m + turn) % members) for m in range(members)])
        other = got if other is None else other + got

    block = jax.ShapeDtypeStruct((rows, moves), jnp.float32)
    scan, alpha, mean, stats = pl.pallas_call(
        functools.partial(local_kernel, members),
        out_shape=(
            block,
            block,
            block,
            jax.ShapeDtypeStruct((blocks * groups, rows, LANES), jnp.float32),
        ),
        in_specs=[VMEM] * 6,
        out_specs=(VMEM,) * 4,
        name="local_scan",
    )(rewards, dones, own, other, discount[None], trace[None])
    stats = lax.all_to_all(stats, ("tm", "games"), 0, 0, tiled=True)
    moves_all = moves * blocks
    returns, advantages, loss = pl.pallas_call(
        functools.partial(
            final_kernel, blocks, groups, float(moves_all), float(moves_all * rows * groups)
        ),
        out_shape=(block, block, jax.ShapeDtypeStruct((1, rows), jnp.float32)),
        in_specs=[VMEM] * 4,
        out_specs=(VMEM,) * 3,
        name="finish",
    )(scan, alpha, mean, stats)
    return returns, advantages, loss


def solution(mesh):
    return jax.shard_map(
        per_device,
        mesh=mesh,
        in_specs=(
            P("games", "tm"),
            P("games", "tm"),
            P("member", "games", "tm"),
            P("games"),
            P("games"),
        ),
        out_specs=(P("games", "tm"), P("games", "tm"), P("member", "games")),
        check_vma=False,
    )
```

```python
import functools

import jax
import jax.numpy as jnp
from jax import lax
from jax.experimental import pallas as pl
from jax.experimental.pallas import tpu as pltpu
from jax.sharding import PartitionSpec as P

LANES = 128
STEPS = tuple(1 << k for k in range(7))
SLOT = 16
GROUPS = LANES // SLOT
VMEM = pl.BlockSpec(memory_space=pltpu.VMEM)
HBM = pl.BlockSpec(memory_space=pltpu.HBM)
VMEM_LIMIT = 4 << 20


def iotas(rows):
    shape = (rows, LANES)
    return (
        lax.broadcasted_iota(jnp.int32, shape, 0),
        lax.broadcasted_iota(jnp.int32, shape, 1),
    )


def spread(column, rows):
    return jnp.broadcast_to(column, (rows, LANES))


def to_column(row, rows):
    sub, lane = iotas(rows)
    padded = jnp.broadcast_to(jnp.pad(row, ((0, 0), (0, LANES - rows))), (rows, LANES))
    return spread(jnp.sum(jnp.where(lane == sub, padded, 0.0), axis=1, keepdims=True), rows)


def at(j):
    return slice(j * LANES, (j + 1) * LANES)


def decay_kernel(
    rewards, dones, own, discount, trace,
    rewards_out, own_out, gates_out, decay_out, alpha_out, boot_out, heads_out, consts_out,
    dones_in, discount_in, trace_in, sems,
):
    rows, moves = dones_in.shape
    tiles = moves // LANES
    sub, lane = iotas(rows)
    pairs = (
        (discount, discount_in),
        (trace, trace_in),
        (dones, dones_in),
        (own, own_out),
        (rewards, rewards_out),
    )
    copies = [pltpu.make_async_copy(*pair, sems.at[k]) for k, pair in enumerate(pairs)]
    for copy in copies:
        copy.start()
    copies[0].wait()
    copies[1].wait()
    disc = to_column(discount_in[...], rows)
    lam = to_column(trace_in[...], rows)
    rate = disc * lam
    boot = disc * (1.0 - lam)
    consts_out[0] = rate
    consts_out[1] = (1.0 - lam) / lam
    copies[2].wait()
    scale = jnp.ones((rows, LANES), jnp.float32)
    saa = jnp.zeros((rows, LANES), jnp.float32)
    for j in reversed(range(tiles)):
        keep = 1.0 - dones_in[:, at(j)].astype(jnp.float32)
        boot_out[:, at(j)] = boot * keep
        a = rate * keep
        for k, step in enumerate(STEPS):
            inside = lane < LANES - step
            gates_out[k, :, at(j)] = jnp.where(inside, a, 0.0)
            a = jnp.where(inside, a * pltpu.roll(a, LANES - step, 1), a)
        head = spread(a[:, :1], rows)
        alpha = a * scale
        decay_out[:, at(j)] = a
        alpha_out[:, at(j)] = alpha
        heads_out[j] = head
        scale = head * scale
        saa += alpha * alpha
    consts_out[2] = scale
    consts_out[3] = spread(jnp.sum(saa, axis=1, keepdims=True), rows)
    copies[3].wait()
    copies[4].wait()


def local_kernel(
    members, rewards, own, other, gates, decay, alpha, boot, heads, consts,
    scan_out, mean_out, stats_out,
):
    rows, moves = rewards.shape
    tiles = moves // LANES
    sub, lane = iotas(rows)
    last_block = lax.axis_index("tm") == lax.axis_size("tm") - 1
    offset_lane = lax.rem(lax.axis_index("games"), GROUPS) * SLOT

    rate, ratio, slope, saa = consts[0], consts[1], consts[2], consts[3]
    own_last = own[:, moves - 1 : moves]
    mean_last = (own_last + other[:, moves - 1 : moves]) / members
    reward_last = rewards[:, moves - 1 : moves]
    guess = jnp.where(last_block, 0.0, spread(mean_last - reward_last, rows) / rate)
    own_guess = jnp.where(last_block, 0.0, spread(own_last - reward_last, rows) / rate)
    gap = own_guess - guess

    zero = jnp.zeros((rows, LANES), jnp.float32)
    carry, ahead = guess, zero
    suu, sua, sqq, sqa = zero, zero, zero, zero
    for j in reversed(range(tiles)):
        mine = own[:, at(j)]
        mean = (mine + other[:, at(j)]) / members
        mean_out[:, at(j)] = mean
        shifted = pltpu.roll(mean, LANES - 1, 1)
        following = jnp.where(lane == LANES - 1, ahead, shifted)
        ahead = shifted
        b = rewards[:, at(j)] + boot[:, at(j)] * following
        for k, step in enumerate(STEPS):
            b = b + gates[k, :, at(j)] * pltpu.roll(b, LANES - step, 1)
        result = b + decay[:, at(j)] * carry
        scan_out[:, at(j)] = result
        carry = spread(b[:, :1], rows) + heads[j] * carry
        weight = alpha[:, at(j)]
        u = result - mean
        q = mine - result - weight * gap
        suu += u * u
        sua += u * weight
        sqq += q * q
        sqa += q * weight

    def total(x):
        return spread(jnp.sum(x, axis=1, keepdims=True), rows)

    entries = (
        carry + ratio * spread(mean_out[:, :1], rows),
        slope,
        guess,
        total(suu),
        total(sua),
        saa,
        own_guess,
        total(sqq),
        total(sqa),
    )
    stats = zero
    for k, entry in enumerate(entries):
        stats = jnp.where(lane == offset_lane + k, entry, stats)
    stats_out[...] = jnp.broadcast_to(stats[None], stats_out.shape)


def final_kernel(
    blocks, groups, moves_all, cells_all, scan, alpha, mean, stats,
    returns_out, adv_out, loss_out, returns, adv, loss, sems,
):
    rows, moves = scan.shape
    tiles = moves // LANES
    sub, lane = iotas(rows)
    block = lax.axis_index("tm")
    group = lax.axis_index("games")
    slot = lax.rem(group, GROUPS) * SLOT

    squares = jnp.zeros((rows, LANES), jnp.float32)
    own_eps = jnp.zeros((rows, LANES), jnp.float32)
    own_loss = jnp.zeros((rows, LANES), jnp.float32)
    for first in range(0, groups, GROUPS):
        last = min(first + GROUPS, groups)
        here = (lane == slot) & (group >= first) & (group < last)
        valid = (lax.rem(lane, SLOT) == 0) & (lane < (last - first) * SLOT)
        ahead = jnp.zeros((rows, LANES), jnp.float32)
        for t in reversed(range(blocks)):
            merged = stats[t * groups + first]
            for g in range(first + 1, last):
                merged = merged + stats[t * groups + g]
            pick = [merged] + [pltpu.roll(merged, LANES - k, 1) for k in range(1, 9)]
            head, slope, guess, suu, sua, saa, own_guess, sqq, sqa = pick
            eps = ahead - guess
            own = ahead - own_guess
            ahead = head + slope * eps
            squares += jnp.where(valid, suu + eps * (2.0 * sua + eps * saa), 0.0)
            own_loss += jnp.where(here, sqq + own * (own * saa - 2.0 * sqa), 0.0)
            own_eps += jnp.where(here & (block == t), eps, 0.0)

    eps = spread(jnp.sum(own_eps, axis=1, keepdims=True), rows)
    total = jnp.sum(jnp.sum(squares, axis=1, keepdims=True), axis=0, keepdims=True)
    norm_scale = jnp.broadcast_to(lax.rsqrt(total / cells_all + 1e-06), (rows, LANES))
    column = spread(jnp.sum(own_loss, axis=1, keepdims=True), rows)
    loss_row = jnp.sum(jnp.where(lane == sub, column, 0.0), axis=0, keepdims=True)
    loss[...] = loss_row[:, :rows] / moves_all
    copies = [pltpu.make_async_copy(loss, loss_out, sems.at[0])]
    copies[0].start()
    parts = 2
    size = tiles // parts
    for part in range(parts):
        for j in range(part * size, (part + 1) * size):
            result = scan[:, at(j)] + alpha[:, at(j)] * eps
            returns[:, at(j)] = result
            adv[:, at(j)] = (result - mean[:, at(j)]) * norm_scale
        span = pl.ds(part * size * LANES, size * LANES)
        for k, (src, dst) in enumerate(((returns, returns_out), (adv, adv_out))):
            copy = pltpu.make_async_copy(
                src.at[:, span], dst.at[:, span], sems.at[1 + 2 * part + k]
            )
            copy.start()
            copies.append(copy)
    for copy in copies:
        copy.wait()


def per_device(rewards, dones, values, discount, trace):
    members = lax.axis_size("member")
    blocks = lax.axis_size("tm")
    groups = lax.axis_size("games")
    own = values[0]
    rows, moves = own.shape
    tiles = moves // LANES
    other = None
    for turn in range(1, members):
        got = lax.ppermute(own, "member", [(m, (m + turn) % members) for m in range(members)])
        other = got if other is None else other + got

    def array(*shape):
        return jax.ShapeDtypeStruct(shape, jnp.float32)

    params = pltpu.CompilerParams(vmem_limit_bytes=VMEM_LIMIT)
    block = array(rows, moves)
    kept_rewards, kept_own, gates, decay, alpha, boot, heads, consts = pl.pallas_call(
        decay_kernel,
        out_shape=(
            block, block, array(len(STEPS), rows, moves), block, block, block,
            array(tiles, rows, LANES), array(4, rows, LANES),
        ),
        in_specs=[HBM] * 5,
        out_specs=(VMEM,) * 8,
        scratch_shapes=[
            pltpu.VMEM((rows, moves), jnp.int32),
            pltpu.VMEM((1, rows), jnp.float32),
            pltpu.VMEM((1, rows), jnp.float32),
            pltpu.SemaphoreType.DMA((5,)),
        ],
        compiler_params=params,
        cost_estimate=pl.CostEstimate(flops=4000000, bytes_accessed=2000000, transcendentals=0),
        name="decay_scan",
    )(
        *(
            pltpu.with_memory_space_constraint(x, pltpu.HBM)
            for x in (rewards, dones, own, discount[None], trace[None])
        )
    )
    scan, mean, stats = pl.pallas_call(
        functools.partial(local_kernel, members),
        out_shape=(block, block, array(blocks * groups, rows, LANES)),
        in_specs=[VMEM] * 9,
        out_specs=(VMEM,) * 3,
        compiler_params=params,
        name="local_scan",
    )(kept_rewards, kept_own, other, gates, decay, alpha, boot, heads, consts)
    stats = lax.all_to_all(stats, ("tm", "games"), 0, 0, tiled=True)
    moves_all = moves * blocks
    returns, advantages, loss = pl.pallas_call(
        functools.partial(
            final_kernel, blocks, groups, float(moves_all), float(moves_all * rows * groups)
        ),
        out_shape=(block, block, array(1, rows)),
        in_specs=[VMEM] * 4,
        out_specs=(HBM,) * 3,
        scratch_shapes=[
            pltpu.VMEM((rows, moves), jnp.float32),
            pltpu.VMEM((rows, moves), jnp.float32),
            pltpu.VMEM((1, rows), jnp.float32),
            pltpu.SemaphoreType.DMA((5,)),
        ],
        compiler_params=params,
        name="finish",
    )(scan, alpha, mean, stats)
    return returns, advantages, loss


def solution(mesh):
    return jax.shard_map(
        per_device,
        mesh=mesh,
        in_specs=(
            P("games", "tm"),
            P("games", "tm"),
            P("member", "games", "tm"),
            P("games"),
            P("games"),
        ),
        out_specs=(P("games", "tm"), P("games", "tm"), P("member", "games")),
        check_vma=False,
    )
```

```python
import functools

import jax
import jax.numpy as jnp
from jax import lax
from jax.experimental import pallas as pl
from jax.experimental.pallas import tpu as pltpu
from jax.sharding import PartitionSpec as P

LANES = 128
STEPS = tuple(1 << k for k in range(7))
SLOT = 16
LOSSES = 6
VMEM = pl.BlockSpec(memory_space=pltpu.VMEM)
HBM = pl.BlockSpec(memory_space=pltpu.HBM)
VMEM_LIMIT = 4 << 20


def iotas(rows):
    shape = (rows, LANES)
    return (
        lax.broadcasted_iota(jnp.int32, shape, 0),
        lax.broadcasted_iota(jnp.int32, shape, 1),
    )


def spread(column, rows):
    return jnp.broadcast_to(column, (rows, LANES))


def to_column(row, rows):
    sub, lane = iotas(rows)
    padded = jnp.broadcast_to(jnp.pad(row, ((0, 0), (0, LANES - rows))), (rows, LANES))
    return spread(jnp.sum(jnp.where(lane == sub, padded, 0.0), axis=1, keepdims=True), rows)


def at(j):
    return slice(j * LANES, (j + 1) * LANES)


def decay_kernel(
    rewards, dones, own, discount, trace,
    rewards_out, own_out, gates_out, decay_out, alpha_out, boot_out, heads_out, consts_out,
    dones_in, discount_in, trace_in, sems,
):
    rows, moves = dones_in.shape
    tiles = moves // LANES
    sub, lane = iotas(rows)
    pairs = (
        (discount, discount_in),
        (trace, trace_in),
        (dones, dones_in),
        (own, own_out),
        (rewards, rewards_out),
    )
    copies = [pltpu.make_async_copy(*pair, sems.at[k]) for k, pair in enumerate(pairs)]
    for copy in copies:
        copy.start()
    copies[0].wait()
    copies[1].wait()
    disc = to_column(discount_in[...], rows)
    lam = to_column(trace_in[...], rows)
    rate = disc * lam
    boot = disc * (1.0 - lam)
    consts_out[0] = rate
    consts_out[1] = (1.0 - lam) / lam
    copies[2].wait()
    scale = jnp.ones((rows, LANES), jnp.float32)
    saa = jnp.zeros((rows, LANES), jnp.float32)
    for j in reversed(range(tiles)):
        keep = 1.0 - dones_in[:, at(j)].astype(jnp.float32)
        boot_out[:, at(j)] = boot * keep
        a = rate * keep
        for k, step in enumerate(STEPS):
            inside = lane < LANES - step
            gates_out[k, :, at(j)] = jnp.where(inside, a, 0.0)
            a = jnp.where(inside, a * pltpu.roll(a, LANES - step, 1), a)
        head = spread(a[:, :1], rows)
        alpha = a * scale
        decay_out[:, at(j)] = a
        alpha_out[:, at(j)] = alpha
        heads_out[j] = head
        scale = head * scale
        saa += alpha * alpha
    consts_out[2] = scale
    consts_out[3] = spread(jnp.sum(saa, axis=1, keepdims=True), rows)
    copies[3].wait()
    copies[4].wait()


def local_kernel(
    rewards, own, *refs,
):
    members = lax.axis_size("member")
    others, (gates, decay, alpha, boot, heads, consts, scan_out, mean_out, stats_out) = (
        refs[: members - 1],
        refs[members - 1 :],
    )
    rows, moves = rewards.shape
    tiles = moves // LANES
    sub, lane = iotas(rows)
    block, blocks = lax.axis_index("tm"), lax.axis_size("tm")
    me = lax.axis_index("member")
    first = (lax.rem(lax.axis_index("games"), LANES // (blocks * SLOT)) * blocks + block) * SLOT

    def mean_of(parts):
        return sum(parts[1:], parts[0]) / members

    def guess_of(value):
        found = spread(value - rewards[:, moves - 1 : moves], rows) / rate
        return jnp.where(block == blocks - 1, 0.0, found)

    rate, ratio, slope, saa = consts[0], consts[1], consts[2], consts[3]
    lasts = [ref[:, moves - 1 : moves] for ref in (own, *others)]
    guess = guess_of(mean_of(lasts))
    guesses = [guess_of(last) for last in lasts]

    zero = jnp.zeros((rows, LANES), jnp.float32)
    carry, ahead = guess, zero
    suu, sua = zero, zero
    sqq, sqa = [zero] * members, [zero] * members
    for j in reversed(range(tiles)):
        parts = [ref[:, at(j)] for ref in (own, *others)]
        mean = mean_of(parts)
        mean_out[:, at(j)] = mean
        shifted = pltpu.roll(mean, LANES - 1, 1)
        following = jnp.where(lane == LANES - 1, ahead, shifted)
        ahead = shifted
        b = rewards[:, at(j)] + boot[:, at(j)] * following
        for k, step in enumerate(STEPS):
            b = b + gates[k, :, at(j)] * pltpu.roll(b, LANES - step, 1)
        result = b + decay[:, at(j)] * carry
        scan_out[:, at(j)] = result
        carry = spread(b[:, :1], rows) + heads[j] * carry
        weight = alpha[:, at(j)]
        u = result - mean
        suu += u * u
        sua += u * weight
        for m, part in enumerate(parts):
            q = part - result - weight * (guesses[m] - guess)
            sqq[m] += q * q
            sqa[m] += q * weight

    def total(x):
        return spread(jnp.sum(x, axis=1, keepdims=True), rows)

    entries = [carry + ratio * spread(mean_out[:, :1], rows), slope, guess]
    entries += [total(suu), total(sua), saa]
    stats = zero
    for k, entry in enumerate(entries):
        stats = jnp.where(lane == first + k, entry, stats)
    for m in range(members):
        at_lane = first + LOSSES + 3 * lax.rem(me + members - m, members)
        for k, entry in enumerate((guesses[m], total(sqq[m]), total(sqa[m]))):
            stats = jnp.where(lane == at_lane + k, entry, stats)
    stats_out[...] = stats


def chain(stats, blocks, picks):
    ahead = jnp.zeros_like(stats)
    for t in reversed(range(blocks)):
        moved = [pltpu.roll(stats, (LANES - t * SLOT - k) % LANES, 1) for k in range(picks)]
        eps = ahead - moved[2]
        yield t, ahead, eps, moved
        ahead = moved[0] + moved[1] * eps


def returns_kernel(
    moves_all, scan, alpha, mean, stats, returns_out, loss_out, raw_out, returns, loss, sems
):
    rows, moves = scan.shape
    tiles = moves // LANES
    sub, lane = iotas(rows)
    blocks, members = lax.axis_size("tm"), lax.axis_size("member")
    block, me = lax.axis_index("tm"), lax.axis_index("member")
    first = lax.rem(lax.axis_index("games"), LANES // (blocks * SLOT)) * blocks * SLOT
    zero = jnp.zeros((rows, LANES), jnp.float32)
    own_eps, own_loss = zero, zero
    for t, ahead, eps, moved in chain(stats[...], blocks, LOSSES + 3 * members):
        saa = moved[5]
        own_eps += jnp.where((lane == first) & (block == t), eps, 0.0)
        for m in range(members):
            guess, sqq, sqa = moved[LOSSES + 3 * m : LOSSES + 3 * m + 3]
            off = ahead - guess
            term = sqq + off * (off * saa - 2.0 * sqa)
            own_loss += jnp.where((lane == first) & (me == m), term, 0.0)
    eps = spread(jnp.sum(own_eps, axis=1, keepdims=True), rows)
    for j in range(tiles):
        result = scan[:, at(j)] + alpha[:, at(j)] * eps
        returns[:, at(j)] = result
        raw_out[:, at(j)] = result - mean[:, at(j)]
    column = spread(jnp.sum(own_loss, axis=1, keepdims=True), rows)
    loss_row = jnp.sum(jnp.where(lane == sub, column, 0.0), axis=0, keepdims=True)
    loss[...] = loss_row[:, :rows] / moves_all
    copies = [
        pltpu.make_async_copy(returns, returns_out, sems.at[0]),
        pltpu.make_async_copy(loss, loss_out, sems.at[1]),
    ]
    for copy in copies:
        copy.start()
    for copy in copies:
        copy.wait()


def scale_kernel(cells_all, raw, *refs):
    *stats, adv_out, adv, sems = refs
    rows, moves = raw.shape
    tiles = moves // LANES
    sub, lane = iotas(rows)
    blocks = lax.axis_size("tm")
    head = lax.rem(lane, blocks * SLOT) == 0
    squares = jnp.zeros((rows, LANES), jnp.float32)
    for ref in stats:
        for n in range(ref.shape[0]):
            for t, ahead, eps, moved in chain(ref[n], blocks, LOSSES):
                suu, sua, saa = moved[3:LOSSES]
                squares += jnp.where(head, suu + eps * (2.0 * sua + eps * saa), 0.0)
    total = jnp.sum(jnp.sum(squares, axis=1, keepdims=True), axis=0, keepdims=True)
    norm_scale = jnp.broadcast_to(lax.rsqrt(total / cells_all + 1e-06), (rows, LANES))
    for j in range(tiles):
        adv[:, at(j)] = raw[:, at(j)] * norm_scale
    copy = pltpu.make_async_copy(adv, adv_out, sems.at[0])
    copy.start()
    copy.wait()


def exchange(value, axis, bit):
    names = ("tm", "games", "member")
    sizes = [lax.axis_size(name) for name in names]
    pairs = []
    for t in range(sizes[0]):
        for g in range(sizes[1]):
            for m in range(sizes[2]):
                to = [t, g, (m + 1) % sizes[2]]
                to[names.index(axis)] ^= bit
                pairs.append(
                    ((t * sizes[1] + g) * sizes[2] + m, (to[0] * sizes[1] + to[1]) * sizes[2] + to[2])
                )
    return lax.ppermute(value, names, pairs)


def bits(count):
    return [1 << k for k in range(count.bit_length() - 1)]


def per_device(rewards, dones, values, discount, trace):
    members = lax.axis_size("member")
    blocks = lax.axis_size("tm")
    groups = lax.axis_size("games")
    own = values[0]
    rows, moves = own.shape
    tiles = moves // LANES
    others = [
        lax.ppermute(own, "member", [(m, (m + turn) % members) for m in range(members)])
        for turn in range(members - 1, 0, -1)
    ]

    def array(*shape):
        return jax.ShapeDtypeStruct(shape, jnp.float32)

    params = pltpu.CompilerParams(vmem_limit_bytes=VMEM_LIMIT)
    block = array(rows, moves)
    kept_rewards, kept_own, gates, decay, alpha, boot, heads, consts = pl.pallas_call(
        decay_kernel,
        out_shape=(
            block, block, array(len(STEPS), rows, moves), block, block, block,
            array(tiles, rows, LANES), array(4, rows, LANES),
        ),
        in_specs=[HBM] * 5,
        out_specs=(VMEM,) * 8,
        scratch_shapes=[
            pltpu.VMEM((rows, moves), jnp.int32),
            pltpu.VMEM((1, rows), jnp.float32),
            pltpu.VMEM((1, rows), jnp.float32),
            pltpu.SemaphoreType.DMA((5,)),
        ],
        compiler_params=params,
        cost_estimate=pl.CostEstimate(flops=4000000, bytes_accessed=2000000, transcendentals=0),
        name="decay_scan",
    )(
        *(
            pltpu.with_memory_space_constraint(x, pltpu.HBM)
            for x in (rewards, dones, own, discount[None], trace[None])
        )
    )
    scan, mean, stats = pl.pallas_call(
        local_kernel,
        out_shape=(block, block, array(rows, LANES)),
        in_specs=[VMEM] * (members + 7),
        out_specs=(VMEM,) * 3,
        compiler_params=params,
        name="local_scan",
    )(kept_rewards, kept_own, *others, gates, decay, alpha, boot, heads, consts)

    for bit in bits(blocks):
        stats = stats + exchange(stats, "tm", bit)
    moves_all = moves * blocks
    returns, loss, raw = pl.pallas_call(
        functools.partial(returns_kernel, float(moves_all)),
        out_shape=(block, array(1, rows), block),
        in_specs=[VMEM] * 4,
        out_specs=(HBM, HBM, VMEM),
        scratch_shapes=[
            pltpu.VMEM((rows, moves), jnp.float32),
            pltpu.VMEM((1, rows), jnp.float32),
            pltpu.SemaphoreType.DMA((2,)),
        ],
        compiler_params=params,
        cost_estimate=pl.CostEstimate(flops=2000000, bytes_accessed=1000000, transcendentals=0),
        name="write_returns",
    )(scan, alpha, mean, stats)
    packed = LANES // (blocks * SLOT)
    for bit in bits(min(groups, packed)):
        stats = stats + exchange(stats, "games", bit)
    stats = [stats[None]]
    for bit in bits(groups)[len(bits(packed)) :]:
        held = stats[0] if len(stats) == 1 else jnp.concatenate(stats)
        stats = [held, exchange(held, "games", bit)]
    advantages = pl.pallas_call(
        functools.partial(scale_kernel, float(moves_all * rows * groups)),
        out_shape=block,
        in_specs=[VMEM] * (1 + len(stats)),
        out_specs=HBM,
        scratch_shapes=[pltpu.VMEM((rows, moves), jnp.float32), pltpu.SemaphoreType.DMA((1,))],
        compiler_params=params,
        name="scale",
    )(raw, *stats)
    return returns, advantages, loss


def solution(mesh):
    return jax.shard_map(
        per_device,
        mesh=mesh,
        in_specs=(
            P("games", "tm"),
            P("games", "tm"),
            P("member", "games", "tm"),
            P("games"),
            P("games"),
        ),
        out_specs=(P("games", "tm"), P("games", "tm"), P("member", "games")),
        check_vma=False,
    )
```

```python
import functools

import jax
import jax.numpy as jnp
from jax import lax
from jax.experimental import pallas as pl
from jax.experimental.pallas import tpu as pltpu
from jax.sharding import PartitionSpec as P

LANES = 128
SUBLANES = 8
CHUNK = LANES // SUBLANES
PITCH = CHUNK + 1
DEPTH = SUBLANES * PITCH
SLOT = 16
GUESSES = 3
SUMS = 8
LOSSES = SUMS + 3
VMEM = pl.BlockSpec(memory_space=pltpu.VMEM)
HBM = pl.BlockSpec(memory_space=pltpu.HBM)
VMEM_LIMIT = 4 << 20


def iotas(rows):
    shape = (rows, LANES)
    return (
        lax.broadcasted_iota(jnp.int32, shape, 0),
        lax.broadcasted_iota(jnp.int32, shape, 1),
    )


def spread(column, rows):
    return jnp.broadcast_to(column, (rows, LANES))


def at(j):
    return slice(j * LANES, (j + 1) * LANES)


def turn(ref, block, tiles):
    flat = jnp.concatenate(tiles, axis=0).T
    for s in range(SUBLANES):
        start = block * DEPTH + s * PITCH
        ref[start : start + CHUNK, :] = flat[s * CHUNK : (s + 1) * CHUNK]


def chunk_rows(ref, block):
    starts = [block * DEPTH + s * PITCH for s in range(SUBLANES)]
    return [ref[start : start + CHUNK, :] for start in starts]


def strip(block, v):
    return pl.ds(block * DEPTH + v, SUBLANES, stride=PITCH)


def from_next(moved, edge, fill):
    following = moved[1:] + [fill]
    return [jnp.where(edge, far, near) for near, far in zip(moved, following)]


def next_chunk(blocks, rows, fill):
    sub, lane = iotas(SUBLANES)
    up = [pltpu.roll(x, SUBLANES - 1, 0) for x in blocks]
    across = from_next([pltpu.roll(x, LANES - rows, 1) for x in up], lane >= LANES - rows, fill)
    return [jnp.where(sub == SUBLANES - 1, far, near) for near, far in zip(up, across)]


def tree_sum(terms):
    while len(terms) > 1:
        odd = terms[-1:] if len(terms) % 2 else []
        terms = [x + y for x, y in zip(terms[::2], terms[1::2])] + odd
    return terms[0]


def product(terms):
    while len(terms) > 1:
        odd = terms[-1:] if len(terms) % 2 else []
        terms = [x * y for x, y in zip(terms[::2], terms[1::2])] + odd
    return terms[0]


def chunks_on(x):
    return [pltpu.roll(x, SUBLANES - k, 0) for k in range(1, SUBLANES)]


def tiles_on(x, rows):
    return [pltpu.roll(x, LANES - k * rows, 1) for k in range(1, LANES // rows)]


def spans(x, onward, place, count):
    one = jnp.ones_like(x)
    run, between = one, []
    for k in range(1, count):
        between.append(jnp.where(place + k < count, run, 0.0))
        run = run * onward[k - 1]
    after = product([jnp.where(place + k < count, onward[k - 1], 1.0) for k in range(1, count)])
    before = product([jnp.where(place >= k, onward[count - k - 1], 1.0) for k in range(1, count)])
    return between, after, before, x * run


def per_row(column, rows):
    sub, lane = iotas(rows)
    picked = jnp.where(lax.rem(lane, rows) == sub, column, 0.0)
    return jnp.broadcast_to(jnp.sum(picked, axis=0, keepdims=True), (SUBLANES, LANES))


def decay_kernel(
    rewards, dones, own, discount, trace,
    own_out, rewards_turned, own_turned, decay_out, reach_out, alpha_turned,
    chunk_out, tile_out, inside_out, after_out, consts_out, squares_out,
    rewards_in, dones_in, discount_in, trace_in, work, sems,
):
    rows, moves = dones_in.shape
    group = LANES // rows
    count = moves // (LANES * group)
    sub, lane = iotas(SUBLANES)
    pairs = (
        (discount, discount_in),
        (trace, trace_in),
        (dones, dones_in),
        (own, own_out),
        (rewards, rewards_in),
    )
    copies = [pltpu.make_async_copy(*pair, sems.at[k]) for k, pair in enumerate(pairs)]
    for copy in copies:
        copy.start()

    def across(row):
        row = jnp.pad(row, ((0, 0), (0, LANES - rows)))
        row = jnp.broadcast_to(row, (SUBLANES, LANES))
        return tree_sum([row] + tiles_on(row, rows))

    copies[0].wait()
    copies[1].wait()
    disc, lam = across(discount_in[...]), across(trace_in[...])
    rate = disc * lam
    consts_out[0] = rate
    consts_out[1] = (1.0 - lam) / lam
    copies[2].wait()
    for b in range(count):
        tiles = [dones_in[:, at(b * group + t)].astype(jnp.float32) for t in range(group)]
        turn(work, b, tiles)
    insides, lasts, befores, wholes = [], [], [], []
    for b in range(count):
        reach = None
        for v in reversed(range(CHUNK)):
            a = rate * (1.0 - work[strip(b, v), :])
            reach = a if reach is None else a * reach
            decay_out[b, v] = a
            reach_out[b, v] = reach
        between, inside, before, whole = spans(reach, chunks_on(reach), sub, SUBLANES)
        for k, gate in enumerate(between):
            chunk_out[b, k] = gate
        chunk_out[b, SUBLANES - 1] = before
        for k, gate in enumerate(chunks_on(before)):
            chunk_out[b, SUBLANES + k] = gate
        place = lane // rows
        between, last, before, whole = spans(whole, tiles_on(whole, rows), place, group)
        for k, gate in enumerate(between):
            tile_out[b, k] = gate
        tile_out[b, group - 1] = before
        for k, gate in enumerate(tiles_on(before, rows)):
            tile_out[b, group + k] = gate
        inside_out[b] = inside
        insides.append(inside)
        lasts.append(last)
        wholes.append(whole)
    squares = jnp.zeros((SUBLANES, LANES), jnp.float32)
    beyond = jnp.ones((SUBLANES, LANES), jnp.float32)
    for b in reversed(range(count)):
        after_out[b, 0] = lasts[b]
        after_out[b, 1] = wholes[b]
        after = insides[b] * lasts[b] * beyond
        after_out[b, 2] = after
        beyond = beyond * wholes[b]
        for v in range(CHUNK):
            alpha = reach_out[b, v] * after
            alpha_turned[strip(b, v), :] = alpha
            squares += alpha * alpha
            if b == 0 and v == 0:
                consts_out[2] = alpha
    squares_out[...] = squares
    copies[3].wait()
    copies[4].wait()
    for k, ref in ((3, rewards_in), (4, own_out)):
        consts_out[k] = per_row(spread(ref[:, moves - 1 : moves], rows), rows)
    for src, dst in ((own_out, own_turned), (rewards_in, rewards_turned)):
        for b in range(count):
            turn(dst, b, [src[:, at(b * group + t)] for t in range(group)])


def local_kernel(rewards, own, *refs):
    members = lax.axis_size("member")
    others, refs = refs[: members - 1], refs[members - 1 :]
    decay, reach, chunk_gates, tile_gates, insides, afters, consts, squares, *refs = refs
    scan_turned, stats_out, sums, folds, *works = refs
    rows, moves = others[0].shape
    group = LANES // rows
    count = moves // (LANES * group)
    sub, lane = iotas(SUBLANES)
    block, blocks = lax.axis_index("tm"), lax.axis_size("tm")
    me = lax.axis_index("member")
    first = (lax.rem(lax.axis_index("games"), LANES // (blocks * SLOT)) * blocks + block) * SLOT
    rate, ratio, slope, last_reward, last_own = (consts[k] for k in range(5))
    values = [own, *works]
    for b in range(count):
        for src, dst in zip(others, works):
            turn(dst, b, [src[:, at(b * group + t)] for t in range(group)])

    def mean_of(parts):
        return sum(parts[1:], parts[0]) / members

    def guess_of(value):
        return jnp.where(block == blocks - 1, 0.0, (value - last_reward) / rate)

    lasts = [last_own]
    lasts += [per_row(spread(ref[:, moves - 1 : moves], rows), rows) for ref in others]
    guess = guess_of(mean_of(lasts))
    guesses = [guess_of(last) for last in lasts]

    zero = jnp.zeros((SUBLANES, LANES), jnp.float32)

    def mean_at(b, v):
        return mean_of([ref[strip(b, v), :] for ref in values])

    followers = next_chunk([mean_at(b, 0) for b in range(count)], rows, zero)
    withins, tiles = [], []
    for b in range(count):
        following, total = followers[b], None
        for v in reversed(range(CHUNK)):
            a = decay[b, v]
            x = rewards[strip(b, v), :] + ratio * a * following
            following = mean_at(b, v)
            total = x if total is None else x + a * total
            sums[b, v] = total
        moved = chunks_on(total)
        withins.append(tree_sum([chunk_gates[b, k] * x for k, x in enumerate(moved)]))
        around = [total] + moved
        tiles.append(
            tree_sum([chunk_gates[b, SUBLANES - 1 + k] * x for k, x in enumerate(around)])
        )
    beyond = zero
    carries = [None] * count
    for b in reversed(range(count)):
        moved = tiles_on(tiles[b], rows)
        onward = tree_sum([tile_gates[b, k] * x for k, x in enumerate(moved)])
        onward = onward + afters[b, 0] * beyond
        carries[b] = withins[b] + insides[b] * onward + afters[b, 2] * guess
        if b:
            around = [tiles[b]] + moved
            whole = tree_sum([tile_gates[b, group - 1 + k] * x for k, x in enumerate(around)])
            beyond = whole + afters[b, 1] * beyond

    suu, sua = zero, zero
    sqq, sqa = [zero] * members, [zero] * members
    for b in range(count):
        carry, after = carries[b], afters[b, 2]
        own_carries = [carry + after * (own_guess - guess) for own_guess in guesses]
        part_ua, part_qa = zero, [zero] * members
        for v in range(CHUNK):
            weight = reach[b, v]
            partial = sums[b, v]
            result = partial + weight * carry
            scan_turned[strip(b, v), :] = result
            parts = [ref[strip(b, v), :] for ref in values]
            mean = mean_of(parts)
            if b == 0 and v == 0:
                head = result + ratio * mean
            u = result - mean
            suu += u * u
            part_ua += u * weight
            for m, part in enumerate(parts):
                q = part - partial - weight * own_carries[m]
                sqq[m] += q * q
                part_qa[m] += q * weight
        sua += part_ua * after
        for m in range(members):
            sqa[m] += part_qa[m] * after

    def by_member(entries, m):
        found = entries[0]
        for turn_of in range(1, members):
            found = jnp.where(lax.rem(me + turn_of, members) == m, entries[turn_of], found)
        return found

    held = jnp.where(sub == 0, head, zero)
    singles = [slope, guess] + [by_member(guesses, m) for m in range(members)]
    for k, entry in enumerate(singles):
        held = jnp.where(sub == 1 + k, jnp.broadcast_to(entry[:1], held.shape), held)
    held = jnp.where(lane < rows, held, 0.0)
    totals = [suu, sua, squares[...]]
    for m in range(members):
        totals += [by_member(sqq, m), by_member(sqa, m)]
    totals += [zero] * (SUBLANES - len(totals))
    for k, entry in enumerate(totals):
        folds[k * (SUBLANES + 1) : k * (SUBLANES + 1) + SUBLANES, :] = entry
    folded = tree_sum(
        [folds[pl.ds(s, SUBLANES, stride=SUBLANES + 1), :] for s in range(SUBLANES)]
    )
    flat = jnp.concatenate([held, folded], axis=0).T
    per_game = tree_sum([flat[t * rows : (t + 1) * rows] for t in range(group)])
    padded = jnp.pad(per_game, ((0, 0), (0, LANES - SLOT)))
    stats_out[...] = pltpu.roll(padded, first, 1)


def chain(stats, blocks, picks):
    ahead = jnp.zeros_like(stats)
    for t in reversed(range(blocks)):
        moved = [pltpu.roll(stats, (LANES - t * SLOT - k) % LANES, 1) for k in range(picks)]
        eps = ahead - moved[2]
        yield t, ahead, eps, moved
        ahead = moved[0] + moved[1] * eps


def returns_kernel(
    moves_all, scan, alpha, stats, *refs
):
    members = lax.axis_size("member")
    values, (returns_out, loss_out, raw_out, returns, loss, sems) = refs[:members], refs[members:]
    rows, moves = values[0].shape
    group = LANES // rows
    count = moves // (LANES * group)
    sub, lane = iotas(rows)
    blocks = lax.axis_size("tm")
    block, me = lax.axis_index("tm"), lax.axis_index("member")
    first = lax.rem(lax.axis_index("games"), LANES // (blocks * SLOT)) * blocks * SLOT
    zero = jnp.zeros((rows, LANES), jnp.float32)
    own_eps, own_loss = zero, zero
    for t, ahead, eps, moved in chain(stats[...], blocks, LOSSES + 2 * members):
        saa = moved[SUMS + 2]
        own_eps += jnp.where((lane == first) & (block == t), eps, 0.0)
        for m in range(members):
            sqq, sqa = moved[LOSSES + 2 * m : LOSSES + 2 * m + 2]
            guess = moved[GUESSES + m]
            off = ahead - guess
            term = sqq + off * (off * saa - 2.0 * sqa)
            own_loss += jnp.where((lane == first) & (me == m), term, 0.0)
    eps = spread(jnp.sum(own_eps, axis=1, keepdims=True), rows)
    eps = per_row(eps, rows)[:1]
    for b in range(count):
        pairs = zip(chunk_rows(scan, b), chunk_rows(alpha, b))
        flat = jnp.concatenate([part + weight * eps for part, weight in pairs], axis=0).T
        for t in range(group):
            j = b * group + t
            result = flat[t * rows : (t + 1) * rows]
            returns[:, at(j)] = result
            parts = [ref[:, at(j)] for ref in values]
            raw_out[:, at(j)] = result - sum(parts[1:], parts[0]) / members
    column = spread(jnp.sum(own_loss, axis=1, keepdims=True), rows)
    loss_row = jnp.sum(jnp.where(lane == sub, column, 0.0), axis=0, keepdims=True)
    loss[...] = loss_row[:, :rows] / moves_all
    copies = [
        pltpu.make_async_copy(returns, returns_out, sems.at[0]),
        pltpu.make_async_copy(loss, loss_out, sems.at[1]),
    ]
    for copy in copies:
        copy.start()
    for copy in copies:
        copy.wait()


def scale_kernel(cells_all, raw, *refs):
    *stats, adv_out, adv, sems = refs
    rows, moves = raw.shape
    tiles = moves // LANES
    sub, lane = iotas(rows)
    blocks = lax.axis_size("tm")
    head = lax.rem(lane, blocks * SLOT) == 0
    squares = jnp.zeros((rows, LANES), jnp.float32)
    for ref in stats:
        for n in range(ref.shape[0]):
            for t, ahead, eps, moved in chain(ref[n], blocks, LOSSES):
                suu, sua, saa = moved[SUMS:LOSSES]
                squares += jnp.where(head, suu + eps * (2.0 * sua + eps * saa), 0.0)
    total = jnp.sum(jnp.sum(squares, axis=1, keepdims=True), axis=0, keepdims=True)
    norm_scale = jnp.broadcast_to(lax.rsqrt(total / cells_all + 1e-06), (rows, LANES))
    for j in range(tiles):
        adv[:, at(j)] = raw[:, at(j)] * norm_scale
    copy = pltpu.make_async_copy(adv, adv_out, sems.at[0])
    copy.start()
    copy.wait()


def exchange(value, axis, bit):
    names = ("tm", "games", "member")
    sizes = [lax.axis_size(name) for name in names]
    pairs = []
    for t in range(sizes[0]):
        for g in range(sizes[1]):
            for m in range(sizes[2]):
                to = [t, g, (m + 1) % sizes[2]]
                to[names.index(axis)] ^= bit
                pairs.append(
                    ((t * sizes[1] + g) * sizes[2] + m, (to[0] * sizes[1] + to[1]) * sizes[2] + to[2])
                )
    return lax.ppermute(value, names, pairs)


def bits(count):
    return [1 << k for k in range(count.bit_length() - 1)]


def per_device(rewards, dones, values, discount, trace):
    members = lax.axis_size("member")
    blocks = lax.axis_size("tm")
    groups = lax.axis_size("games")
    own = values[0]
    rows, moves = own.shape
    others = [
        lax.ppermute(own, "member", [(m, (m + turn) % members) for m in range(members)])
        for turn in range(members - 1, 0, -1)
    ]

    def array(*shape):
        return jax.ShapeDtypeStruct(shape, jnp.float32)

    params = pltpu.CompilerParams(vmem_limit_bytes=VMEM_LIMIT)
    block = array(rows, moves)
    group = LANES // rows
    count = moves // (LANES * group)
    flat = array(count * DEPTH, LANES)
    strips = array(count, CHUNK, SUBLANES, LANES)
    row = pltpu.VMEM((1, rows), jnp.float32)
    kept_own, *kept = pl.pallas_call(
        decay_kernel,
        out_shape=(
            block, flat, flat, strips, strips, flat,
            array(count, 2 * SUBLANES - 1, SUBLANES, LANES),
            array(count, 2 * group - 1, SUBLANES, LANES),
            array(count, SUBLANES, LANES),
            array(count, 3, SUBLANES, LANES),
            array(5, SUBLANES, LANES),
            array(SUBLANES, LANES),
        ),
        in_specs=[HBM] * 5,
        out_specs=(VMEM,) * 12,
        scratch_shapes=[
            pltpu.VMEM((rows, moves), jnp.float32),
            pltpu.VMEM((rows, moves), jnp.int32),
            row,
            row,
            pltpu.VMEM((count * DEPTH, LANES), jnp.float32),
            pltpu.SemaphoreType.DMA((5,)),
        ],
        compiler_params=params,
        cost_estimate=pl.CostEstimate(flops=4000000, bytes_accessed=2000000, transcendentals=0),
        name="decay_scan",
    )(
        *(
            pltpu.with_memory_space_constraint(x, pltpu.HBM)
            for x in (rewards, dones, own, discount[None], trace[None])
        )
    )
    rewards_turned, own_turned, decay, reach, alpha, *gates = kept
    scan, stats = pl.pallas_call(
        local_kernel,
        out_shape=(flat, array(rows, LANES)),
        in_specs=[VMEM] * (members + 9),
        out_specs=(VMEM,) * 2,
        scratch_shapes=[
            pltpu.VMEM((count, CHUNK, SUBLANES, LANES), jnp.float32),
            pltpu.VMEM((SUBLANES * (SUBLANES + 1), LANES), jnp.float32),
        ]
        + [pltpu.VMEM((count * DEPTH, LANES), jnp.float32)] * (members - 1),
        compiler_params=params,
        name="local_scan",
    )(rewards_turned, own_turned, *others, decay, reach, *gates)

    for bit in bits(blocks):
        stats = stats + exchange(stats, "tm", bit)
    moves_all = moves * blocks
    returns, loss, raw = pl.pallas_call(
        functools.partial(returns_kernel, float(moves_all)),
        out_shape=(block, array(1, rows), block),
        in_specs=[VMEM] * (3 + members),
        out_specs=(HBM, HBM, VMEM),
        scratch_shapes=[
            pltpu.VMEM((rows, moves), jnp.float32),
            pltpu.VMEM((1, rows), jnp.float32),
            pltpu.SemaphoreType.DMA((2,)),
        ],
        compiler_params=params,
        cost_estimate=pl.CostEstimate(flops=2000000, bytes_accessed=1000000, transcendentals=0),
        name="write_returns",
    )(scan, alpha, stats, kept_own, *others)
    packed = LANES // (blocks * SLOT)
    for bit in bits(min(groups, packed)):
        stats = stats + exchange(stats, "games", bit)
    stats = [stats[None]]
    for bit in bits(groups)[len(bits(packed)) :]:
        held = stats[0] if len(stats) == 1 else jnp.concatenate(stats)
        stats = [held, exchange(held, "games", bit)]
    advantages = pl.pallas_call(
        functools.partial(scale_kernel, float(moves_all * rows * groups)),
        out_shape=block,
        in_specs=[VMEM] * (1 + len(stats)),
        out_specs=HBM,
        scratch_shapes=[pltpu.VMEM((rows, moves), jnp.float32), pltpu.SemaphoreType.DMA((1,))],
        compiler_params=params,
        name="scale",
    )(raw, *stats)
    return returns, advantages, loss


def solution(mesh):
    return jax.shard_map(
        per_device,
        mesh=mesh,
        in_specs=(
            P("games", "tm"),
            P("games", "tm"),
            P("member", "games", "tm"),
            P("games"),
            P("games"),
        ),
        out_specs=(P("games", "tm"), P("games", "tm"), P("member", "games")),
        check_vma=False,
    )
```

```python
import functools

import jax
import jax.numpy as jnp
from jax import lax
from jax.experimental import pallas as pl
from jax.experimental.pallas import tpu as pltpu
from jax.sharding import PartitionSpec as P

LANES = 128
SUBLANES = 8
CHUNK = LANES // SUBLANES
PITCH = CHUNK + 1
DEPTH = SUBLANES * PITCH
SLOT = 16
GUESSES = 3
SUMS = 8
LOSSES = SUMS + 3
VMEM = pl.BlockSpec(memory_space=pltpu.VMEM)
HBM = pl.BlockSpec(memory_space=pltpu.HBM)
VMEM_LIMIT = 4 << 20


def iotas(rows):
    shape = (rows, LANES)
    return (
        lax.broadcasted_iota(jnp.int32, shape, 0),
        lax.broadcasted_iota(jnp.int32, shape, 1),
    )


def spread(column, rows):
    return jnp.broadcast_to(column, (rows, LANES))


def at(j):
    return slice(j * LANES, (j + 1) * LANES)


def turn(ref, block, tiles):
    flat = jnp.concatenate(tiles, axis=0).T
    for s in range(SUBLANES):
        start = block * DEPTH + s * PITCH
        ref[start : start + CHUNK, :] = flat[s * CHUNK : (s + 1) * CHUNK]


def chunk_rows(ref, block):
    starts = [block * DEPTH + s * PITCH for s in range(SUBLANES)]
    return [ref[start : start + CHUNK, :] for start in starts]


def strip(block, v):
    return pl.ds(block * DEPTH + v, SUBLANES, stride=PITCH)


def from_next(moved, edge, fill):
    following = moved[1:] + [fill]
    return [jnp.where(edge, far, near) for near, far in zip(moved, following)]


def next_chunk(blocks, rows, fill):
    sub, lane = iotas(SUBLANES)
    up = [pltpu.roll(x, SUBLANES - 1, 0) for x in blocks]
    across = from_next([pltpu.roll(x, LANES - rows, 1) for x in up], lane >= LANES - rows, fill)
    return [jnp.where(sub == SUBLANES - 1, far, near) for near, far in zip(up, across)]


def tree_sum(terms):
    while len(terms) > 1:
        odd = terms[-1:] if len(terms) % 2 else []
        terms = [x + y for x, y in zip(terms[::2], terms[1::2])] + odd
    return terms[0]


def product(terms):
    while len(terms) > 1:
        odd = terms[-1:] if len(terms) % 2 else []
        terms = [x * y for x, y in zip(terms[::2], terms[1::2])] + odd
    return terms[0]


def chunks_on(x):
    return [pltpu.roll(x, SUBLANES - k, 0) for k in range(1, SUBLANES)]


def tiles_on(x, rows):
    return [pltpu.roll(x, LANES - k * rows, 1) for k in range(1, LANES // rows)]


def spans(x, onward, place, count):
    one = jnp.ones_like(x)
    run, wrapped = one, one
    between, after, parts = [], [], []
    for k in range(1, count):
        inside = place + k < count
        value = onward[k - 1]
        between.append(jnp.where(inside, run, 0.0))
        after.append(jnp.where(inside, value, 1.0))
        parts.append((inside, run, wrapped))
        run = run * value
        wrapped = wrapped * jnp.where(inside, 1.0, value)
    here = x * wrapped
    before = [wrapped] + [jnp.where(inside, here * ran, gone) for inside, ran, gone in parts]
    return between, product(after), x * run, before


def per_row(column, rows):
    sub, lane = iotas(rows)
    picked = jnp.where(lax.rem(lane, rows) == sub, column, 0.0)
    return jnp.broadcast_to(jnp.sum(picked, axis=0, keepdims=True), (SUBLANES, LANES))


def decay_kernel(
    rewards, dones, own, discount, trace,
    own_out, rewards_turned, own_turned, decay_out, reach_out,
    powers_out, consts_out,
    rewards_in, dones_in, discount_in, trace_in, work, sems,
):
    rows, moves = dones_in.shape
    group = LANES // rows
    count = moves // (LANES * group)
    sub, lane = iotas(SUBLANES)
    pairs = (
        (discount, discount_in),
        (trace, trace_in),
        (dones, dones_in),
        (own, own_out),
        (rewards, rewards_in),
    )
    copies = [pltpu.make_async_copy(*pair, sems.at[k]) for k, pair in enumerate(pairs)]
    for copy in copies:
        copy.start()

    def across(row):
        row = jnp.pad(row, ((0, 0), (0, LANES - rows)))
        row = jnp.broadcast_to(row, (SUBLANES, LANES))
        return tree_sum([row] + tiles_on(row, rows))

    copies[0].wait()
    copies[1].wait()
    disc, lam = across(discount_in[...]), across(trace_in[...])
    rate = disc * lam
    consts_out[0] = rate
    consts_out[1] = (1.0 - lam) / lam
    for copy in copies[2:]:
        copy.wait()
    for b in range(count):
        tiles = [dones_in[:, at(b * group + t)].astype(jnp.float32) for t in range(group)]
        turn(work, b, tiles)
    powers = []
    for b in range(count):
        reach, power = None, jnp.zeros((SUBLANES, LANES), jnp.float32)
        for v in reversed(range(CHUNK)):
            a = rate * (1.0 - work[strip(b, v), :])
            reach = a if reach is None else a * reach
            decay_out[b, v] = a
            reach_out[b, v] = reach
            power += reach * reach
        powers.append(power)
    for b in range(count):
        powers_out[b] = powers[b]
    for k, ref in ((2, rewards_in), (3, own_out)):
        consts_out[k] = per_row(spread(ref[:, moves - 1 : moves], rows), rows)
    for src, dst in ((own_out, own_turned), (rewards_in, rewards_turned)):
        for b in range(count):
            turn(dst, b, [src[:, at(b * group + t)] for t in range(group)])


def local_kernel(rewards, own, *refs):
    members = lax.axis_size("member")
    others, refs = refs[: members - 1], refs[members - 1 :]
    decay, reach, powers, consts, scan_out, after_out, stats_out, sums, folds, *works = refs
    rows, moves = others[0].shape
    group = LANES // rows
    count = moves // (LANES * group)
    sub, lane = iotas(SUBLANES)
    block, blocks = lax.axis_index("tm"), lax.axis_size("tm")
    me = lax.axis_index("member")
    first = (lax.rem(lax.axis_index("games"), LANES // (blocks * SLOT)) * blocks + block) * SLOT
    rate, ratio, last_reward, last_own = (consts[k] for k in range(4))
    values = [own, *works]
    for b in range(count):
        for src, dst in zip(others, works):
            turn(dst, b, [src[:, at(b * group + t)] for t in range(group)])

    chunk_gates, tile_gates = [], []
    insides, lasts, wholes, afters = [], [], [], [None] * count
    for b in range(count):
        total = reach[b, 0]
        between, inside, whole, before = spans(total, chunks_on(total), sub, SUBLANES)
        chunk_gates.append((between, before))
        insides.append(inside)
        between, last, whole, before = spans(whole, tiles_on(whole, rows), lane // rows, group)
        tile_gates.append((between, before))
        lasts.append(last)
        wholes.append(whole)
    beyond = jnp.ones((SUBLANES, LANES), jnp.float32)
    squares = jnp.zeros((SUBLANES, LANES), jnp.float32)
    for b in reversed(range(count)):
        afters[b] = insides[b] * lasts[b] * beyond
        after_out[b] = afters[b]
        beyond = beyond * wholes[b]
        squares += powers[b] * (afters[b] * afters[b])
    slope = reach[0, 0] * afters[0]

    def mean_of(parts):
        return sum(parts[1:], parts[0]) / members

    def guess_of(value):
        return jnp.where(block == blocks - 1, 0.0, (value - last_reward) / rate)

    ends = [last_own]
    ends += [per_row(spread(ref[:, moves - 1 : moves], rows), rows) for ref in others]
    guess = guess_of(mean_of(ends))
    guesses = [guess_of(end) for end in ends]

    zero = jnp.zeros((SUBLANES, LANES), jnp.float32)

    def mean_at(b, v):
        return mean_of([ref[strip(b, v), :] for ref in values])

    followers = next_chunk([mean_at(b, 0) for b in range(count)], rows, zero)
    withins, tiles = [], []
    for b in range(count):
        following, total = followers[b], None
        for v in reversed(range(CHUNK)):
            a = decay[b, v]
            x = rewards[strip(b, v), :] + ratio * a * following
            following = mean_at(b, v)
            total = x if total is None else x + a * total
            sums[b, v] = total
        moved = chunks_on(total)
        between, before = chunk_gates[b]
        withins.append(tree_sum([gate * x for gate, x in zip(between, moved)]))
        tiles.append(tree_sum([gate * x for gate, x in zip(before, [total] + moved)]))
    beyond = zero
    carries = [None] * count
    for b in reversed(range(count)):
        moved = tiles_on(tiles[b], rows)
        between, before = tile_gates[b]
        onward = tree_sum([gate * x for gate, x in zip(between, moved)]) + lasts[b] * beyond
        carries[b] = withins[b] + insides[b] * onward + afters[b] * guess
        if b:
            whole = tree_sum([gate * x for gate, x in zip(before, [tiles[b]] + moved)])
            beyond = whole + wholes[b] * beyond

    suu, sua = zero, zero
    sqq, sqa = [zero] * members, [zero] * members
    for b in range(count):
        carry, after = carries[b], afters[b]
        own_carries = [carry + after * (own_guess - guess) for own_guess in guesses]
        part_ua, part_qa = zero, [zero] * members
        for v in range(CHUNK):
            weight = reach[b, v]
            partial = sums[b, v]
            result = partial + weight * carry
            scan_out[b, v] = result
            parts = [ref[strip(b, v), :] for ref in values]
            mean = mean_of(parts)
            if b == 0 and v == 0:
                head = result + ratio * mean
            u = result - mean
            suu += u * u
            part_ua += u * weight
            for m, part in enumerate(parts):
                q = part - partial - weight * own_carries[m]
                sqq[m] += q * q
                part_qa[m] += q * weight
        sua += part_ua * after
        for m in range(members):
            sqa[m] += part_qa[m] * after

    def by_member(entries, m):
        found = entries[0]
        for turn_of in range(1, members):
            found = jnp.where(lax.rem(me + turn_of, members) == m, entries[turn_of], found)
        return found

    held = jnp.where(sub == 0, head, zero)
    singles = [slope, guess] + [by_member(guesses, m) for m in range(members)]
    for k, entry in enumerate(singles):
        held = jnp.where(sub == 1 + k, jnp.broadcast_to(entry[:1], held.shape), held)
    held = jnp.where(lane < rows, held, 0.0)
    totals = [suu, sua, squares]
    for m in range(members):
        totals += [by_member(sqq, m), by_member(sqa, m)]
    totals += [zero] * (SUBLANES - len(totals))
    for k, entry in enumerate(totals):
        folds[k * (SUBLANES + 1) : k * (SUBLANES + 1) + SUBLANES, :] = entry
    folded = tree_sum(
        [folds[pl.ds(s, SUBLANES, stride=SUBLANES + 1), :] for s in range(SUBLANES)]
    )
    flat = jnp.concatenate([held, folded], axis=0).T
    per_game = tree_sum([flat[t * rows : (t + 1) * rows] for t in range(group)])
    padded = jnp.pad(per_game, ((0, 0), (0, LANES - SLOT)))
    stats_out[...] = pltpu.roll(padded, first, 1)


def chain(stats, blocks, picks):
    ahead = jnp.zeros_like(stats)
    for t in reversed(range(blocks)):
        moved = {k: pltpu.roll(stats, (LANES - t * SLOT - k) % LANES, 1) for k in picks}
        eps = ahead - moved[2]
        yield t, ahead, eps, moved
        ahead = moved[0] + moved[1] * eps


def squares_of(stats, blocks):
    sub, lane = iotas(stats.shape[0])
    found = jnp.zeros_like(stats)
    for t, ahead, eps, moved in chain(stats, blocks, (0, 1, 2, SUMS, SUMS + 1, SUMS + 2)):
        suu, sua, saa = (moved[SUMS + k] for k in range(3))
        found += suu + eps * (2.0 * sua + eps * saa)
    return jnp.where(lax.rem(lane, blocks * SLOT) == 0, found, 0.0)


def returns_kernel(
    moves_all, scan, reach, afters, stats, *refs
):
    members = lax.axis_size("member")
    values, refs = refs[:members], refs[members:]
    returns_out, loss_out, raw_out, squares_out, returns, loss, work, sems = refs
    rows, moves = values[0].shape
    group = LANES // rows
    count = moves // (LANES * group)
    sub, lane = iotas(rows)
    blocks = lax.axis_size("tm")
    block, me = lax.axis_index("tm"), lax.axis_index("member")
    first = lax.rem(lax.axis_index("games"), LANES // (blocks * SLOT)) * blocks * SLOT
    zero = jnp.zeros((rows, LANES), jnp.float32)
    own_eps, own_loss = zero, zero
    squares_out[...] = squares_of(stats[...], blocks)
    for t, ahead, eps, moved in chain(stats[...], blocks, range(LOSSES + 2 * members)):
        saa = moved[SUMS + 2]
        own_eps += jnp.where((lane == first) & (block == t), eps, 0.0)
        for m in range(members):
            sqq, sqa = moved[LOSSES + 2 * m], moved[LOSSES + 2 * m + 1]
            guess = moved[GUESSES + m]
            off = ahead - guess
            term = sqq + off * (off * saa - 2.0 * sqa)
            own_loss += jnp.where((lane == first) & (me == m), term, 0.0)
    eps = spread(jnp.sum(own_eps, axis=1, keepdims=True), rows)
    eps = per_row(eps, rows)
    for b in range(count):
        error = afters[b] * eps
        for v in range(CHUNK):
            work[strip(b, v), :] = scan[b, v] + reach[b, v] * error
        flat = jnp.concatenate(chunk_rows(work, b), axis=0).T
        for t in range(group):
            j = b * group + t
            result = flat[t * rows : (t + 1) * rows]
            returns[:, at(j)] = result
            parts = [ref[:, at(j)] for ref in values]
            raw_out[:, at(j)] = result - sum(parts[1:], parts[0]) / members
    column = spread(jnp.sum(own_loss, axis=1, keepdims=True), rows)
    loss_row = jnp.sum(jnp.where(lane == sub, column, 0.0), axis=0, keepdims=True)
    loss[...] = loss_row[:, :rows] / moves_all
    copies = [
        pltpu.make_async_copy(returns, returns_out, sems.at[0]),
        pltpu.make_async_copy(loss, loss_out, sems.at[1]),
    ]
    for copy in copies:
        copy.start()
    for copy in copies:
        copy.wait()


def scale_kernel(cells_all, raw, squares, *refs):
    *stats, adv_out, adv, rows_in, sems = refs
    rows, moves = raw.shape
    tiles = moves // LANES
    found = squares[...]
    for ref in stats:
        for n in range(ref.shape[0]):
            found += squares_of(ref[n], lax.axis_size("tm"))
    rows_in[...] = found
    found = tree_sum([jnp.broadcast_to(rows_in[s : s + 1, :], found.shape) for s in range(rows)])
    total = spread(jnp.sum(found, axis=1, keepdims=True), rows)
    norm_scale = lax.rsqrt(total / cells_all + 1e-06)
    for j in range(tiles):
        adv[:, at(j)] = raw[:, at(j)] * norm_scale
    copy = pltpu.make_async_copy(adv, adv_out, sems.at[0])
    copy.start()
    copy.wait()


def exchange(value, axis, bit):
    names = ("tm", "games", "member")
    sizes = [lax.axis_size(name) for name in names]
    pairs = []
    for t in range(sizes[0]):
        for g in range(sizes[1]):
            for m in range(sizes[2]):
                to = [t, g, (m + 1) % sizes[2]]
                to[names.index(axis)] ^= bit
                pairs.append(
                    ((t * sizes[1] + g) * sizes[2] + m, (to[0] * sizes[1] + to[1]) * sizes[2] + to[2])
                )
    return lax.ppermute(value, names, pairs)


def bits(count):
    return [1 << k for k in range(count.bit_length() - 1)]


def per_device(rewards, dones, values, discount, trace):
    members = lax.axis_size("member")
    blocks = lax.axis_size("tm")
    groups = lax.axis_size("games")
    own = values[0]
    rows, moves = own.shape
    others = [
        lax.ppermute(own, "member", [(m, (m + turn) % members) for m in range(members)])
        for turn in range(members - 1, 0, -1)
    ]

    def array(*shape):
        return jax.ShapeDtypeStruct(shape, jnp.float32)

    params = pltpu.CompilerParams(vmem_limit_bytes=VMEM_LIMIT)
    block = array(rows, moves)
    group = LANES // rows
    count = moves // (LANES * group)
    flat = array(count * DEPTH, LANES)
    strips = array(count, CHUNK, SUBLANES, LANES)
    row = pltpu.VMEM((1, rows), jnp.float32)
    kept_own, *kept = pl.pallas_call(
        decay_kernel,
        out_shape=(
            block, flat, flat, strips, strips,
            array(count, SUBLANES, LANES),
            array(4, SUBLANES, LANES),
        ),
        in_specs=[HBM] * 5,
        out_specs=(VMEM,) * 7,
        scratch_shapes=[
            pltpu.VMEM((rows, moves), jnp.float32),
            pltpu.VMEM((rows, moves), jnp.int32),
            row,
            row,
            pltpu.VMEM((count * DEPTH, LANES), jnp.float32),
            pltpu.SemaphoreType.DMA((5,)),
        ],
        compiler_params=params,
        cost_estimate=pl.CostEstimate(flops=4000000, bytes_accessed=2000000, transcendentals=0),
        name="decay_scan",
    )(
        *(
            pltpu.with_memory_space_constraint(x, pltpu.HBM)
            for x in (rewards, dones, own, discount[None], trace[None])
        )
    )
    rewards_turned, own_turned, decay, reach, powers, consts = kept
    scan, afters, stats = pl.pallas_call(
        local_kernel,
        out_shape=(strips, array(count, SUBLANES, LANES), array(rows, LANES)),
        in_specs=[VMEM] * (members + 5),
        out_specs=(VMEM,) * 3,
        scratch_shapes=[
            pltpu.VMEM((count, CHUNK, SUBLANES, LANES), jnp.float32),
            pltpu.VMEM((SUBLANES * (SUBLANES + 1), LANES), jnp.float32),
        ]
        + [pltpu.VMEM((count * DEPTH, LANES), jnp.float32)] * (members - 1),
        compiler_params=params,
        name="local_scan",
    )(rewards_turned, own_turned, *others, decay, reach, powers, consts)

    for bit in bits(blocks):
        stats = stats + exchange(stats, "tm", bit)
    packed = LANES // (blocks * SLOT)
    for bit in bits(min(groups, packed)):
        stats = stats + exchange(stats, "games", bit)
    held, received = stats[None], []
    for bit in bits(groups)[len(bits(packed)) :]:
        if received:
            held = jnp.concatenate([held, received[-1]])
        received.append(exchange(held, "games", bit))
    moves_all = moves * blocks
    returns, loss, raw, squares = pl.pallas_call(
        functools.partial(returns_kernel, float(moves_all)),
        out_shape=(block, array(1, rows), block, array(rows, LANES)),
        in_specs=[VMEM] * (4 + members),
        out_specs=(HBM, HBM, VMEM, VMEM),
        scratch_shapes=[
            pltpu.VMEM((rows, moves), jnp.float32),
            pltpu.VMEM((1, rows), jnp.float32),
            pltpu.VMEM((count * DEPTH, LANES), jnp.float32),
            pltpu.SemaphoreType.DMA((2,)),
        ],
        compiler_params=params,
        cost_estimate=pl.CostEstimate(flops=2000000, bytes_accessed=1000000, transcendentals=0),
        name="write_returns",
    )(scan, reach, afters, stats, kept_own, *others)
    advantages = pl.pallas_call(
        functools.partial(scale_kernel, float(moves_all * rows * groups)),
        out_shape=block,
        in_specs=[VMEM] * (2 + len(received)),
        out_specs=HBM,
        scratch_shapes=[
            pltpu.VMEM((rows, moves), jnp.float32),
            pltpu.VMEM((rows, LANES), jnp.float32),
            pltpu.SemaphoreType.DMA((1,)),
        ],
        compiler_params=params,
        name="scale",
    )(raw, squares, *received)
    return returns, advantages, loss


def solution(mesh):
    return jax.shard_map(
        per_device,
        mesh=mesh,
        in_specs=(
            P("games", "tm"),
            P("games", "tm"),
            P("member", "games", "tm"),
            P("games"),
            P("games"),
        ),
        out_specs=(P("games", "tm"), P("games", "tm"), P("member", "games")),
        check_vma=False,
    )
```

```python
import functools

import jax
import jax.numpy as jnp
from jax import lax
from jax.experimental import pallas as pl
from jax.experimental.pallas import tpu as pltpu
from jax.sharding import PartitionSpec as P

LANES = 128
SUBLANES = 8
CHUNK = LANES // SUBLANES
PITCH = CHUNK + 1
DEPTH = SUBLANES * PITCH
SLOT = 16
GUESSES = 3
SUMS = 8
LOSSES = SUMS + 3
VMEM = pl.BlockSpec(memory_space=pltpu.VMEM)
HBM = pl.BlockSpec(memory_space=pltpu.HBM)
VMEM_LIMIT = 4 << 20


def iotas(rows):
    shape = (rows, LANES)
    return (
        lax.broadcasted_iota(jnp.int32, shape, 0),
        lax.broadcasted_iota(jnp.int32, shape, 1),
    )


def spread(column, rows):
    return jnp.broadcast_to(column, (rows, LANES))


def at(j):
    return slice(j * LANES, (j + 1) * LANES)


def turn(ref, block, tiles):
    flat = jnp.concatenate(tiles, axis=0).T
    for s in range(SUBLANES):
        start = block * DEPTH + s * PITCH
        ref[start : start + CHUNK, :] = flat[s * CHUNK : (s + 1) * CHUNK]


def chunk_rows(ref, block):
    starts = [block * DEPTH + s * PITCH for s in range(SUBLANES)]
    return [ref[start : start + CHUNK, :] for start in starts]


def strip(block, v):
    return pl.ds(block * DEPTH + v, SUBLANES, stride=PITCH)


def from_next(moved, edge, fill):
    following = moved[1:] + [fill]
    return [jnp.where(edge, far, near) for near, far in zip(moved, following)]


def next_chunk(blocks, rows, fill):
    sub, lane = iotas(SUBLANES)
    up = [pltpu.roll(x, SUBLANES - 1, 0) for x in blocks]
    across = from_next([pltpu.roll(x, LANES - rows, 1) for x in up], lane >= LANES - rows, fill)
    return [jnp.where(sub == SUBLANES - 1, far, near) for near, far in zip(up, across)]


def tree_sum(terms):
    while len(terms) > 1:
        odd = terms[-1:] if len(terms) % 2 else []
        terms = [x + y for x, y in zip(terms[::2], terms[1::2])] + odd
    return terms[0]


def product(terms):
    while len(terms) > 1:
        odd = terms[-1:] if len(terms) % 2 else []
        terms = [x * y for x, y in zip(terms[::2], terms[1::2])] + odd
    return terms[0]


def chunks_on(x):
    return [pltpu.roll(x, SUBLANES - k, 0) for k in range(1, SUBLANES)]


def tiles_on(x, rows):
    return [pltpu.roll(x, LANES - k * rows, 1) for k in range(1, LANES // rows)]


def spans(x, onward, place, count):
    one = jnp.ones_like(x)
    run, wrapped = one, one
    between, parts = [], []
    for k in range(1, count):
        inside = place + k < count
        value = onward[k - 1]
        between.append(jnp.where(inside, run, 0.0))
        parts.append((inside, run, wrapped))
        run = run * jnp.where(inside, value, 1.0)
        wrapped = wrapped * jnp.where(inside, 1.0, value)
    here = x * wrapped
    before = [wrapped] + [jnp.where(inside, here * ran, gone) for inside, ran, gone in parts]
    return between, run, here * run, before


def per_row(column, rows):
    sub, lane = iotas(rows)
    picked = jnp.where(lax.rem(lane, rows) == sub, column, 0.0)
    return jnp.broadcast_to(jnp.sum(picked, axis=0, keepdims=True), (SUBLANES, LANES))


def decay_kernel(
    rewards, dones, own, discount, trace,
    own_out, rewards_turned, own_turned, decay_out, reach_out,
    powers_out, consts_out,
    rewards_in, dones_in, discount_in, trace_in, work, sems,
):
    rows, moves = dones_in.shape
    group = LANES // rows
    count = moves // (LANES * group)
    sub, lane = iotas(SUBLANES)
    pairs = (
        (discount, discount_in),
        (trace, trace_in),
        (dones, dones_in),
        (own, own_out),
        (rewards, rewards_in),
    )
    copies = [pltpu.make_async_copy(*pair, sems.at[k]) for k, pair in enumerate(pairs)]
    for copy in copies:
        copy.start()

    def across(row):
        row = jnp.pad(row, ((0, 0), (0, LANES - rows)))
        row = jnp.broadcast_to(row, (SUBLANES, LANES))
        return tree_sum([row] + tiles_on(row, rows))

    copies[0].wait()
    copies[1].wait()
    disc, lam = across(discount_in[...]), across(trace_in[...])
    rate = disc * lam
    consts_out[0] = rate
    consts_out[1] = (1.0 - lam) / lam
    for copy in copies[2:]:
        copy.wait()
    for b in range(count):
        tiles = [dones_in[:, at(b * group + t)].astype(jnp.float32) for t in range(group)]
        turn(work, b, tiles)
    powers = []
    for b in range(count):
        reach, power = None, jnp.zeros((SUBLANES, LANES), jnp.float32)
        for v in reversed(range(CHUNK)):
            a = rate * (1.0 - work[strip(b, v), :])
            reach = a if reach is None else a * reach
            decay_out[b, v] = a
            reach_out[b, v] = reach
            power += reach * reach
        powers.append(power)
    for b in range(count):
        powers_out[b] = powers[b]
    for k, ref in ((2, rewards_in), (3, own_out)):
        consts_out[k] = per_row(spread(ref[:, moves - 1 : moves], rows), rows)
    for src, dst in ((own_out, own_turned), (rewards_in, rewards_turned)):
        for b in range(count):
            turn(dst, b, [src[:, at(b * group + t)] for t in range(group)])


def local_kernel(rewards, own, *refs):
    members = lax.axis_size("member")
    others, refs = refs[: members - 1], refs[members - 1 :]
    decay, reach, powers, consts, sums, carry_out, after_out, stats_out, folds, *works = refs
    rows, moves = others[0].shape
    group = LANES // rows
    count = moves // (LANES * group)
    sub, lane = iotas(SUBLANES)
    block, blocks = lax.axis_index("tm"), lax.axis_size("tm")
    me = lax.axis_index("member")
    first = (lax.rem(lax.axis_index("games"), LANES // (blocks * SLOT)) * blocks + block) * SLOT
    rate, ratio, last_reward, last_own = (consts[k] for k in range(4))
    values = [own, *works]
    for b in range(count):
        for src, dst in zip(others, works):
            turn(dst, b, [src[:, at(b * group + t)] for t in range(group)])

    chunk_gates, tile_gates = [], []
    insides, lasts, wholes, afters = [], [], [], [None] * count
    for b in range(count):
        total = reach[b, 0]
        between, inside, whole, before = spans(total, chunks_on(total), sub, SUBLANES)
        chunk_gates.append((between, before))
        insides.append(inside)
        between, last, whole, before = spans(whole, tiles_on(whole, rows), lane // rows, group)
        tile_gates.append((between, before))
        lasts.append(last)
        wholes.append(whole)
    beyond = jnp.ones((SUBLANES, LANES), jnp.float32)
    squares = jnp.zeros((SUBLANES, LANES), jnp.float32)
    for b in reversed(range(count)):
        afters[b] = insides[b] * lasts[b] * beyond
        after_out[b] = afters[b]
        beyond = beyond * wholes[b]
        squares += powers[b] * (afters[b] * afters[b])
    slope = reach[0, 0] * afters[0]

    def mean_of(parts):
        return sum(parts[1:], parts[0]) / members

    def guess_of(value):
        return jnp.where(block == blocks - 1, 0.0, (value - last_reward) / rate)

    ends = [last_own]
    ends += [per_row(spread(ref[:, moves - 1 : moves], rows), rows) for ref in others]
    guess = guess_of(mean_of(ends))
    guesses = [guess_of(end) for end in ends]

    zero = jnp.zeros((SUBLANES, LANES), jnp.float32)

    def mean_at(b, v):
        return mean_of([ref[strip(b, v), :] for ref in values])

    followers = next_chunk([mean_at(b, 0) for b in range(count)], rows, zero)
    withins, tiles = [], []
    for b in range(count):
        following, total = followers[b], None
        for v in reversed(range(CHUNK)):
            a = decay[b, v]
            x = rewards[strip(b, v), :] + ratio * a * following
            following = mean_at(b, v)
            total = x if total is None else x + a * total
            sums[b, v] = total
        moved = chunks_on(total)
        between, before = chunk_gates[b]
        withins.append(tree_sum([gate * x for gate, x in zip(between, moved)]))
        tiles.append(tree_sum([gate * x for gate, x in zip(before, [total] + moved)]))
    beyond = zero
    carries = [None] * count
    for b in reversed(range(count)):
        moved = tiles_on(tiles[b], rows)
        between, before = tile_gates[b]
        onward = tree_sum([gate * x for gate, x in zip(between, moved)]) + lasts[b] * beyond
        carries[b] = withins[b] + insides[b] * onward + afters[b] * guess
        if b:
            whole = tree_sum([gate * x for gate, x in zip(before, [tiles[b]] + moved)])
            beyond = whole + wholes[b] * beyond

    head = sums[0, 0] + reach[0, 0] * carries[0] + ratio * mean_at(0, 0)
    total = zero
    sqq, sqa = [zero] * members, [zero] * members
    for b in range(count):
        carry, after = carries[b], afters[b]
        carry_out[b] = carry
        own_carries = [carry + after * (own_guess - guess) for own_guess in guesses]
        part_qa = [zero] * members
        for v in range(CHUNK):
            weight, partial = reach[b, v], sums[b, v]
            error = None
            for m, ref in enumerate(values):
                q = ref[strip(b, v), :] - partial - weight * own_carries[m]
                sqq[m] += q * q
                part_qa[m] += q * weight
                error = q if error is None else error + q
            total += error * error
        for m in range(members):
            sqa[m] += part_qa[m] * after
    suu = total / (members * members)
    sua = -sum(sqa[1:], sqa[0]) / members

    def by_member(entries, m):
        found = entries[0]
        for turn_of in range(1, members):
            found = jnp.where(lax.rem(me + turn_of, members) == m, entries[turn_of], found)
        return found

    held = jnp.where(sub == 0, head, zero)
    singles = [slope, guess] + [by_member(guesses, m) for m in range(members)]
    for k, entry in enumerate(singles):
        held = jnp.where(sub == 1 + k, jnp.broadcast_to(entry[:1], held.shape), held)
    held = jnp.where(lane < rows, held, 0.0)
    totals = [suu, sua, squares]
    for m in range(members):
        totals += [by_member(sqq, m), by_member(sqa, m)]
    totals += [zero] * (SUBLANES - len(totals))
    for k, entry in enumerate(totals):
        folds[k * (SUBLANES + 1) : k * (SUBLANES + 1) + SUBLANES, :] = entry
    folded = tree_sum(
        [folds[pl.ds(s, SUBLANES, stride=SUBLANES + 1), :] for s in range(SUBLANES)]
    )
    flat = jnp.concatenate([held, folded], axis=0).T
    per_game = tree_sum([flat[t * rows : (t + 1) * rows] for t in range(group)])
    padded = jnp.pad(per_game, ((0, 0), (0, LANES - SLOT)))
    stats_out[...] = pltpu.roll(padded, first, 1)


def chain(stats, blocks, picks):
    ahead = jnp.zeros_like(stats)
    for t in reversed(range(blocks)):
        moved = {k: pltpu.roll(stats, (LANES - t * SLOT - k) % LANES, 1) for k in picks}
        eps = ahead - moved[2]
        yield t, ahead, eps, moved
        ahead = moved[0] + moved[1] * eps


def squares_of(stats, blocks):
    sub, lane = iotas(stats.shape[0])
    found = jnp.zeros_like(stats)
    for t, ahead, eps, moved in chain(stats, blocks, (0, 1, 2, SUMS, SUMS + 1, SUMS + 2)):
        suu, sua, saa = (moved[SUMS + k] for k in range(3))
        found += suu + eps * (2.0 * sua + eps * saa)
    return jnp.where(lax.rem(lane, blocks * SLOT) == 0, found, 0.0)


def returns_kernel(
    moves_all, sums, reach, carries, afters, stats, *refs
):
    members = lax.axis_size("member")
    values, refs = refs[:members], refs[members:]
    returns_out, loss_out, raw_out, squares_out, returns, loss, work, sems = refs
    rows, moves = values[0].shape
    group = LANES // rows
    count = moves // (LANES * group)
    sub, lane = iotas(rows)
    blocks = lax.axis_size("tm")
    block, me = lax.axis_index("tm"), lax.axis_index("member")
    first = lax.rem(lax.axis_index("games"), LANES // (blocks * SLOT)) * blocks * SLOT
    zero = jnp.zeros((rows, LANES), jnp.float32)
    own_eps, own_loss = zero, zero
    squares_out[...] = squares_of(stats[...], blocks)
    for t, ahead, eps, moved in chain(stats[...], blocks, range(LOSSES + 2 * members)):
        saa = moved[SUMS + 2]
        own_eps += jnp.where((lane == first) & (block == t), eps, 0.0)
        for m in range(members):
            sqq, sqa = moved[LOSSES + 2 * m], moved[LOSSES + 2 * m + 1]
            guess = moved[GUESSES + m]
            off = ahead - guess
            term = sqq + off * (off * saa - 2.0 * sqa)
            own_loss += jnp.where((lane == first) & (me == m), term, 0.0)
    eps = spread(jnp.sum(own_eps, axis=1, keepdims=True), rows)
    eps = per_row(eps, rows)
    for b in range(count):
        carry = carries[b] + afters[b] * eps
        for v in range(CHUNK):
            work[strip(b, v), :] = sums[b, v] + reach[b, v] * carry
        flat = jnp.concatenate(chunk_rows(work, b), axis=0).T
        for t in range(group):
            j = b * group + t
            result = flat[t * rows : (t + 1) * rows]
            returns[:, at(j)] = result
            parts = [ref[:, at(j)] for ref in values]
            raw_out[:, at(j)] = result - sum(parts[1:], parts[0]) / members
    column = spread(jnp.sum(own_loss, axis=1, keepdims=True), rows)
    loss_row = jnp.sum(jnp.where(lane == sub, column, 0.0), axis=0, keepdims=True)
    loss[...] = loss_row[:, :rows] / moves_all
    copies = [
        pltpu.make_async_copy(returns, returns_out, sems.at[0]),
        pltpu.make_async_copy(loss, loss_out, sems.at[1]),
    ]
    for copy in copies:
        copy.start()
    for copy in copies:
        copy.wait()


def scale_kernel(cells_all, raw, squares, *refs):
    *stats, adv_out, adv, rows_in, sems = refs
    rows, moves = raw.shape
    tiles = moves // LANES
    found = squares[...]
    for ref in stats:
        for n in range(ref.shape[0]):
            found += squares_of(ref[n], lax.axis_size("tm"))
    rows_in[...] = found
    found = tree_sum([jnp.broadcast_to(rows_in[s : s + 1, :], found.shape) for s in range(rows)])
    total = spread(jnp.sum(found, axis=1, keepdims=True), rows)
    norm_scale = lax.rsqrt(total / cells_all + 1e-06)
    for j in range(tiles):
        adv[:, at(j)] = raw[:, at(j)] * norm_scale
    copy = pltpu.make_async_copy(adv, adv_out, sems.at[0])
    copy.start()
    copy.wait()


def exchange(value, axis, bit):
    names = ("tm", "games", "member")
    sizes = [lax.axis_size(name) for name in names]
    pairs = []
    for t in range(sizes[0]):
        for g in range(sizes[1]):
            for m in range(sizes[2]):
                to = [t, g, (m + 1) % sizes[2]]
                to[names.index(axis)] ^= bit
                pairs.append(
                    ((t * sizes[1] + g) * sizes[2] + m, (to[0] * sizes[1] + to[1]) * sizes[2] + to[2])
                )
    return lax.ppermute(value, names, pairs)


def bits(count):
    return [1 << k for k in range(count.bit_length() - 1)]


def per_device(rewards, dones, values, discount, trace):
    members = lax.axis_size("member")
    blocks = lax.axis_size("tm")
    groups = lax.axis_size("games")
    own = values[0]
    rows, moves = own.shape
    others = [
        lax.ppermute(own, "member", [(m, (m + turn) % members) for m in range(members)])
        for turn in range(members - 1, 0, -1)
    ]

    def array(*shape):
        return jax.ShapeDtypeStruct(shape, jnp.float32)

    params = pltpu.CompilerParams(vmem_limit_bytes=VMEM_LIMIT)
    block = array(rows, moves)
    group = LANES // rows
    count = moves // (LANES * group)
    flat = array(count * DEPTH, LANES)
    strips = array(count, CHUNK, SUBLANES, LANES)
    row = pltpu.VMEM((1, rows), jnp.float32)
    kept_own, *kept = pl.pallas_call(
        decay_kernel,
        out_shape=(
            block, flat, flat, strips, strips,
            array(count, SUBLANES, LANES),
            array(4, SUBLANES, LANES),
        ),
        in_specs=[HBM] * 5,
        out_specs=(VMEM,) * 7,
        scratch_shapes=[
            pltpu.VMEM((rows, moves), jnp.float32),
            pltpu.VMEM((rows, moves), jnp.int32),
            row,
            row,
            pltpu.VMEM((count * DEPTH, LANES), jnp.float32),
            pltpu.SemaphoreType.DMA((5,)),
        ],
        compiler_params=params,
        cost_estimate=pl.CostEstimate(flops=4000000, bytes_accessed=2000000, transcendentals=0),
        name="decay_scan",
    )(
        *(
            pltpu.with_memory_space_constraint(x, pltpu.HBM)
            for x in (rewards, dones, own, discount[None], trace[None])
        )
    )
    rewards_turned, own_turned, decay, reach, powers, consts = kept
    sums, carries, afters, stats = pl.pallas_call(
        local_kernel,
        out_shape=(strips, *[array(count, SUBLANES, LANES)] * 2, array(rows, LANES)),
        in_specs=[VMEM] * (members + 5),
        out_specs=(VMEM,) * 4,
        scratch_shapes=[
            pltpu.VMEM((SUBLANES * (SUBLANES + 1), LANES), jnp.float32),
        ]
        + [pltpu.VMEM((count * DEPTH, LANES), jnp.float32)] * (members - 1),
        compiler_params=params,
        name="local_scan",
    )(rewards_turned, own_turned, *others, decay, reach, powers, consts)

    for bit in bits(blocks):
        stats = stats + exchange(stats, "tm", bit)
    packed = LANES // (blocks * SLOT)
    for bit in bits(min(groups, packed)):
        stats = stats + exchange(stats, "games", bit)
    held, received = stats[None], []
    for bit in bits(groups)[len(bits(packed)) :]:
        if received:
            held = jnp.concatenate([held, received[-1]])
        received.append(exchange(held, "games", bit))
    moves_all = moves * blocks
    returns, loss, raw, squares = pl.pallas_call(
        functools.partial(returns_kernel, float(moves_all)),
        out_shape=(block, array(1, rows), block, array(rows, LANES)),
        in_specs=[VMEM] * (5 + members),
        out_specs=(HBM, HBM, VMEM, VMEM),
        scratch_shapes=[
            pltpu.VMEM((rows, moves), jnp.float32),
            pltpu.VMEM((1, rows), jnp.float32),
            pltpu.VMEM((count * DEPTH, LANES), jnp.float32),
            pltpu.SemaphoreType.DMA((2,)),
        ],
        compiler_params=params,
        cost_estimate=pl.CostEstimate(flops=2000000, bytes_accessed=1000000, transcendentals=0),
        name="write_returns",
    )(sums, reach, carries, afters, stats, kept_own, *others)
    advantages = pl.pallas_call(
        functools.partial(scale_kernel, float(moves_all * rows * groups)),
        out_shape=block,
        in_specs=[VMEM] * (2 + len(received)),
        out_specs=HBM,
        scratch_shapes=[
            pltpu.VMEM((rows, moves), jnp.float32),
            pltpu.VMEM((rows, LANES), jnp.float32),
            pltpu.SemaphoreType.DMA((1,)),
        ],
        compiler_params=params,
        name="scale",
    )(raw, squares, *received)
    return returns, advantages, loss


def solution(mesh):
    return jax.shard_map(
        per_device,
        mesh=mesh,
        in_specs=(
            P("games", "tm"),
            P("games", "tm"),
            P("member", "games", "tm"),
            P("games"),
            P("games"),
        ),
        out_specs=(P("games", "tm"), P("games", "tm"), P("member", "games")),
        check_vma=False,
    )
```

```python
import functools

import jax
import jax.numpy as jnp
from jax import lax
from jax.experimental import pallas as pl
from jax.experimental.pallas import tpu as pltpu
from jax.sharding import PartitionSpec as P

LANES = 128
SUBLANES = 8
CHUNK = LANES // SUBLANES
PITCH = CHUNK + 1
DEPTH = SUBLANES * PITCH
SLOT = 16
GUESSES = 3
SUMS = 8
LOSSES = SUMS + 3
VMEM = pl.BlockSpec(memory_space=pltpu.VMEM)
HBM = pl.BlockSpec(memory_space=pltpu.HBM)
VMEM_LIMIT = 4 << 20


def iotas(rows):
    shape = (rows, LANES)
    return (
        lax.broadcasted_iota(jnp.int32, shape, 0),
        lax.broadcasted_iota(jnp.int32, shape, 1),
    )


def spread(column, rows):
    return jnp.broadcast_to(column, (rows, LANES))


def at(j):
    return slice(j * LANES, (j + 1) * LANES)


def turn(ref, block, tiles):
    flat = jnp.concatenate(tiles, axis=0).T
    for s in range(SUBLANES):
        start = block * DEPTH + s * PITCH
        ref[start : start + CHUNK, :] = flat[s * CHUNK : (s + 1) * CHUNK]


def chunk_rows(ref, block):
    starts = [block * DEPTH + s * PITCH for s in range(SUBLANES)]
    return [ref[start : start + CHUNK, :] for start in starts]


def strip(block, v):
    return pl.ds(block * DEPTH + v, SUBLANES, stride=PITCH)


def from_next(moved, edge, fill):
    following = moved[1:] + [fill]
    return [jnp.where(edge, far, near) for near, far in zip(moved, following)]


def next_chunk(blocks, rows, fill):
    sub, lane = iotas(SUBLANES)
    up = [pltpu.roll(x, SUBLANES - 1, 0) for x in blocks]
    across = from_next([pltpu.roll(x, LANES - rows, 1) for x in up], lane >= LANES - rows, fill)
    return [jnp.where(sub == SUBLANES - 1, far, near) for near, far in zip(up, across)]


def tree_sum(terms):
    while len(terms) > 1:
        odd = terms[-1:] if len(terms) % 2 else []
        terms = [x + y for x, y in zip(terms[::2], terms[1::2])] + odd
    return terms[0]


def product(terms):
    while len(terms) > 1:
        odd = terms[-1:] if len(terms) % 2 else []
        terms = [x * y for x, y in zip(terms[::2], terms[1::2])] + odd
    return terms[0]


def chunks_on(x):
    return [pltpu.roll(x, SUBLANES - k, 0) for k in range(1, SUBLANES)]


def tiles_on(x, rows):
    return [pltpu.roll(x, LANES - k * rows, 1) for k in range(1, LANES // rows)]


def spans(x, onward, place, count):
    one = jnp.ones_like(x)
    run, wrapped = one, one
    between, parts = [], []
    for k in range(1, count):
        inside = place + k < count
        value = onward[k - 1]
        between.append(jnp.where(inside, run, 0.0))
        parts.append((inside, run, wrapped))
        run = run * jnp.where(inside, value, 1.0)
        wrapped = wrapped * jnp.where(inside, 1.0, value)
    here = x * wrapped
    before = [wrapped] + [jnp.where(inside, here * ran, gone) for inside, ran, gone in parts]
    return between, run, here * run, before


def per_row(column, rows):
    sub, lane = iotas(rows)
    picked = jnp.where(lax.rem(lane, rows) == sub, column, 0.0)
    return jnp.broadcast_to(jnp.sum(picked, axis=0, keepdims=True), (SUBLANES, LANES))


def decay_kernel(
    rewards, dones, own, discount, trace,
    own_out, rewards_turned, own_turned, decay_out, reach_out,
    powers_out, consts_out,
    rewards_in, dones_in, discount_in, trace_in, work, sems,
):
    rows, moves = dones_in.shape
    group = LANES // rows
    count = moves // (LANES * group)
    sub, lane = iotas(SUBLANES)
    pairs = (
        (discount, discount_in),
        (trace, trace_in),
        (dones, dones_in),
        (own, own_out),
        (rewards, rewards_in),
    )
    copies = [pltpu.make_async_copy(*pair, sems.at[k]) for k, pair in enumerate(pairs)]
    for copy in copies:
        copy.start()

    def across(row):
        row = jnp.pad(row, ((0, 0), (0, LANES - rows)))
        row = jnp.broadcast_to(row, (SUBLANES, LANES))
        return tree_sum([row] + tiles_on(row, rows))

    copies[0].wait()
    copies[1].wait()
    disc, lam = across(discount_in[...]), across(trace_in[...])
    rate = disc * lam
    consts_out[0] = rate
    consts_out[1] = (1.0 - lam) / lam
    for copy in copies[2:]:
        copy.wait()
    for b in range(count):
        tiles = [dones_in[:, at(b * group + t)].astype(jnp.float32) for t in range(group)]
        turn(work, b, tiles)
    powers = []
    for b in range(count):
        reach, power = None, jnp.zeros((SUBLANES, LANES), jnp.float32)
        for v in reversed(range(CHUNK)):
            a = rate * (1.0 - work[strip(b, v), :])
            reach = a if reach is None else a * reach
            decay_out[b, v] = a
            reach_out[b, v] = reach
            power += reach * reach
        powers.append(power)
    for b in range(count):
        powers_out[b] = powers[b]
    for k, ref in ((2, rewards_in), (3, own_out)):
        consts_out[k] = per_row(spread(ref[:, moves - 1 : moves], rows), rows)
    for src, dst in ((own_out, own_turned), (rewards_in, rewards_turned)):
        for b in range(count):
            turn(dst, b, [src[:, at(b * group + t)] for t in range(group)])


def local_kernel(rewards, own, *refs):
    members = lax.axis_size("member")
    others, refs = refs[: members - 1], refs[members - 1 :]
    decay, reach, powers, consts, sums, carry_out, after_out, stats_out, folds, *works = refs
    rows, moves = others[0].shape
    group = LANES // rows
    count = moves // (LANES * group)
    sub, lane = iotas(SUBLANES)
    block, blocks = lax.axis_index("tm"), lax.axis_size("tm")
    me = lax.axis_index("member")
    first = (lax.rem(lax.axis_index("games"), LANES // (blocks * SLOT)) * blocks + block) * SLOT
    rate, ratio, last_reward, last_own = (consts[k] for k in range(4))
    values = [own, *works]
    for b in range(count):
        for src, dst in zip(others, works):
            turn(dst, b, [src[:, at(b * group + t)] for t in range(group)])

    chunk_gates, tile_gates = [], []
    insides, lasts, wholes, afters = [], [], [], [None] * count
    for b in range(count):
        total = reach[b, 0]
        between, inside, whole, before = spans(total, chunks_on(total), sub, SUBLANES)
        chunk_gates.append((between, before))
        insides.append(inside)
        between, last, whole, before = spans(whole, tiles_on(whole, rows), lane // rows, group)
        tile_gates.append((between, before))
        lasts.append(last)
        wholes.append(whole)
    beyond = jnp.ones((SUBLANES, LANES), jnp.float32)
    squares = jnp.zeros((SUBLANES, LANES), jnp.float32)
    for b in reversed(range(count)):
        afters[b] = insides[b] * lasts[b] * beyond
        after_out[b] = afters[b]
        beyond = beyond * wholes[b]
        squares += powers[b] * (afters[b] * afters[b])
    slope = reach[0, 0] * afters[0]

    def mean_of(parts):
        return sum(parts[1:], parts[0]) / members

    def guess_of(value):
        return jnp.where(block == blocks - 1, 0.0, (value - last_reward) / rate)

    ends = [last_own]
    ends += [per_row(spread(ref[:, moves - 1 : moves], rows), rows) for ref in others]
    guess = guess_of(mean_of(ends))
    guesses = [guess_of(end) for end in ends]

    zero = jnp.zeros((SUBLANES, LANES), jnp.float32)

    def mean_at(b, v):
        return mean_of([ref[strip(b, v), :] for ref in values])

    followers = next_chunk([mean_at(b, 0) for b in range(count)], rows, zero)
    withins, tiles = [], []
    for b in range(count):
        following, total = followers[b], None
        for v in reversed(range(CHUNK)):
            a = decay[b, v]
            x = rewards[strip(b, v), :] + ratio * a * following
            following = mean_at(b, v)
            total = x if total is None else x + a * total
            sums[b, v] = total
        moved = chunks_on(total)
        between, before = chunk_gates[b]
        withins.append(tree_sum([gate * x for gate, x in zip(between, moved)]))
        tiles.append(tree_sum([gate * x for gate, x in zip(before, [total] + moved)]))
    beyond = zero
    carries = [None] * count
    for b in reversed(range(count)):
        moved = tiles_on(tiles[b], rows)
        between, before = tile_gates[b]
        onward = tree_sum([gate * x for gate, x in zip(between, moved)]) + lasts[b] * beyond
        carries[b] = withins[b] + insides[b] * onward + afters[b] * guess
        if b:
            whole = tree_sum([gate * x for gate, x in zip(before, [tiles[b]] + moved)])
            beyond = whole + wholes[b] * beyond

    head = sums[0, 0] + reach[0, 0] * carries[0] + ratio * mean_at(0, 0)
    total = zero
    sqq, sqa = [zero] * members, [zero] * members
    for b in range(count):
        carry, after = carries[b], afters[b]
        carry_out[b] = carry
        own_carries = [carry + after * (own_guess - guess) for own_guess in guesses]
        part_qa = [zero] * members
        for v in range(CHUNK):
            weight, partial = reach[b, v], sums[b, v]
            error = None
            for m, ref in enumerate(values):
                q = ref[strip(b, v), :] - partial - weight * own_carries[m]
                sqq[m] += q * q
                part_qa[m] += q * weight
                error = q if error is None else error + q
            total += error * error
        for m in range(members):
            sqa[m] += part_qa[m] * after
    suu = total / (members * members)
    sua = -sum(sqa[1:], sqa[0]) / members

    def by_member(entries, m):
        found = entries[0]
        for turn_of in range(1, members):
            found = jnp.where(lax.rem(me + turn_of, members) == m, entries[turn_of], found)
        return found

    held = jnp.where(sub == 0, head, zero)
    singles = [slope, guess] + [by_member(guesses, m) for m in range(members)]
    for k, entry in enumerate(singles):
        held = jnp.where(sub == 1 + k, jnp.broadcast_to(entry[:1], held.shape), held)
    held = jnp.where(lane < rows, held, 0.0)
    totals = [suu, sua, squares]
    for m in range(members):
        totals += [by_member(sqq, m), by_member(sqa, m)]
    totals += [zero] * (SUBLANES - len(totals))
    for k, entry in enumerate(totals):
        folds[k * (SUBLANES + 1) : k * (SUBLANES + 1) + SUBLANES, :] = entry
    folded = tree_sum(
        [folds[pl.ds(s, SUBLANES, stride=SUBLANES + 1), :] for s in range(SUBLANES)]
    )
    flat = jnp.concatenate([held, folded], axis=0).T
    per_game = tree_sum([flat[t * rows : (t + 1) * rows] for t in range(group)])
    padded = jnp.pad(per_game, ((0, 0), (0, LANES - SLOT)))
    stats_out[...] = pltpu.roll(padded, first, 1)


def chain(stats, blocks, picks):
    ahead = jnp.zeros_like(stats)
    for t in reversed(range(blocks)):
        moved = {k: pltpu.roll(stats, (LANES - t * SLOT - k) % LANES, 1) for k in picks}
        eps = ahead - moved[2]
        yield t, ahead, eps, moved
        ahead = moved[0] + moved[1] * eps


def squares_of(stats, blocks):
    sub, lane = iotas(stats.shape[0])
    found = jnp.zeros_like(stats)
    for t, ahead, eps, moved in chain(stats, blocks, (0, 1, 2, SUMS, SUMS + 1, SUMS + 2)):
        suu, sua, saa = (moved[SUMS + k] for k in range(3))
        found += suu + eps * (2.0 * sua + eps * saa)
    return jnp.where(lax.rem(lane, blocks * SLOT) == 0, found, 0.0)


def returns_kernel(
    moves_all, sums, reach, carries, afters, stats, *refs
):
    members = lax.axis_size("member")
    values, refs = refs[:members], refs[members:]
    returns_out, loss_out, raw_out, squares_out, returns, loss, work, sems = refs
    rows, moves = values[0].shape
    group = LANES // rows
    count = moves // (LANES * group)
    sub, lane = iotas(rows)
    blocks = lax.axis_size("tm")
    block, me = lax.axis_index("tm"), lax.axis_index("member")
    first = lax.rem(lax.axis_index("games"), LANES // (blocks * SLOT)) * blocks * SLOT
    zero = jnp.zeros((rows, LANES), jnp.float32)
    own_eps, own_loss = zero, zero
    squares_out[...] = squares_of(stats[...], blocks)
    for t, ahead, eps, moved in chain(stats[...], blocks, range(LOSSES + 2 * members)):
        saa = moved[SUMS + 2]
        own_eps += jnp.where((lane == first) & (block == t), eps, 0.0)
        for m in range(members):
            sqq, sqa = moved[LOSSES + 2 * m], moved[LOSSES + 2 * m + 1]
            guess = moved[GUESSES + m]
            off = ahead - guess
            term = sqq + off * (off * saa - 2.0 * sqa)
            own_loss += jnp.where((lane == first) & (me == m), term, 0.0)
    eps = spread(jnp.sum(own_eps, axis=1, keepdims=True), rows)
    eps = per_row(eps, rows)
    for b in range(count):
        carry = carries[b] + afters[b] * eps
        for v in range(CHUNK):
            work[strip(b, v), :] = sums[b, v] + reach[b, v] * carry
        flat = jnp.concatenate(chunk_rows(work, b), axis=0).T
        for t in range(group):
            j = b * group + t
            result = flat[t * rows : (t + 1) * rows]
            returns[:, at(j)] = result
            parts = [ref[:, at(j)] for ref in values]
            raw_out[:, at(j)] = result - sum(parts[1:], parts[0]) / members
    column = spread(jnp.sum(own_loss, axis=1, keepdims=True), rows)
    loss_row = jnp.sum(jnp.where(lane == sub, column, 0.0), axis=0, keepdims=True)
    loss[...] = loss_row[:, :rows] / moves_all
    copies = [
        pltpu.make_async_copy(returns, returns_out, sems.at[0]),
        pltpu.make_async_copy(loss, loss_out, sems.at[1]),
    ]
    for copy in copies:
        copy.start()
    for copy in copies:
        copy.wait()


def scale_kernel(cells_all, raw, squares, *refs):
    *stats, adv_out, adv, rows_in, sems = refs
    rows, moves = raw.shape
    tiles = moves // LANES
    found = squares[...]
    for ref in stats:
        for n in range(ref.shape[0]):
            found += squares_of(ref[n], lax.axis_size("tm"))
    rows_in[...] = found
    found = tree_sum([jnp.broadcast_to(rows_in[s : s + 1, :], found.shape) for s in range(rows)])
    total = spread(jnp.sum(found, axis=1, keepdims=True), rows)
    norm_scale = lax.rsqrt(total / cells_all + 1e-06)
    for j in range(tiles):
        adv[:, at(j)] = raw[:, at(j)] * norm_scale
    copy = pltpu.make_async_copy(adv, adv_out, sems.at[0])
    copy.start()
    copy.wait()


def exchange(value, axis, bit):
    names = ("tm", "games", "member")
    sizes = [lax.axis_size(name) for name in names]
    pairs = []
    for t in range(sizes[0]):
        for g in range(sizes[1]):
            for m in range(sizes[2]):
                to = [t, g, (m + 1) % sizes[2]]
                to[names.index(axis)] ^= bit
                pairs.append(
                    ((t * sizes[1] + g) * sizes[2] + m, (to[0] * sizes[1] + to[1]) * sizes[2] + to[2])
                )
    return lax.ppermute(value, names, pairs)


def bits(count):
    return [1 << k for k in range(count.bit_length() - 1)]


def per_device(rewards, dones, values, discount, trace):
    members = lax.axis_size("member")
    blocks = lax.axis_size("tm")
    groups = lax.axis_size("games")
    own = values[0]
    rows, moves = own.shape
    others = [
        lax.ppermute(own, "member", [(m, (m + turn) % members) for m in range(members)])
        for turn in range(members - 1, 0, -1)
    ]

    def array(*shape):
        return jax.ShapeDtypeStruct(shape, jnp.float32)

    params = pltpu.CompilerParams(vmem_limit_bytes=VMEM_LIMIT)
    block = array(rows, moves)
    group = LANES // rows
    count = moves // (LANES * group)
    flat = array(count * DEPTH, LANES)
    strips = array(count, CHUNK, SUBLANES, LANES)
    row = pltpu.VMEM((1, rows), jnp.float32)
    kept_own, *kept = pl.pallas_call(
        decay_kernel,
        out_shape=(
            block, flat, flat, strips, strips,
            array(count, SUBLANES, LANES),
            array(4, SUBLANES, LANES),
        ),
        in_specs=[HBM] * 5,
        out_specs=(VMEM,) * 7,
        scratch_shapes=[
            pltpu.VMEM((rows, moves), jnp.float32),
            pltpu.VMEM((rows, moves), jnp.int32),
            row,
            row,
            pltpu.VMEM((count * DEPTH, LANES), jnp.float32),
            pltpu.SemaphoreType.DMA((5,)),
        ],
        compiler_params=params,
        cost_estimate=pl.CostEstimate(flops=4000000, bytes_accessed=2000000, transcendentals=0),
        name="decay_scan",
    )(
        *(
            pltpu.with_memory_space_constraint(x, pltpu.HBM)
            for x in (rewards, dones, own, discount[None], trace[None])
        )
    )
    rewards_turned, own_turned, decay, reach, powers, consts = kept
    sums, carries, afters, stats = pl.pallas_call(
        local_kernel,
        out_shape=(strips, *[array(count, SUBLANES, LANES)] * 2, array(rows, LANES)),
        in_specs=[VMEM] * (members + 5),
        out_specs=(VMEM,) * 4,
        scratch_shapes=[
            pltpu.VMEM((SUBLANES * (SUBLANES + 1), LANES), jnp.float32),
        ]
        + [pltpu.VMEM((count * DEPTH, LANES), jnp.float32)] * (members - 1),
        compiler_params=params,
        name="local_scan",
    )(rewards_turned, own_turned, *others, decay, reach, powers, consts)

    stats = sum((exchange(stats, "tm", mask) for mask in range(1, blocks)), stats)
    packed = LANES // (blocks * SLOT)
    for bit in bits(min(groups, packed)):
        stats = stats + exchange(stats, "games", bit)
    held, received = stats[None], []
    for bit in bits(groups)[len(bits(packed)) :]:
        if received:
            held = jnp.concatenate([held, received[-1]])
        received.append(exchange(held, "games", bit))
    moves_all = moves * blocks
    returns, loss, raw, squares = pl.pallas_call(
        functools.partial(returns_kernel, float(moves_all)),
        out_shape=(block, array(1, rows), block, array(rows, LANES)),
        in_specs=[VMEM] * (5 + members),
        out_specs=(HBM, HBM, VMEM, VMEM),
        scratch_shapes=[
            pltpu.VMEM((rows, moves), jnp.float32),
            pltpu.VMEM((1, rows), jnp.float32),
            pltpu.VMEM((count * DEPTH, LANES), jnp.float32),
            pltpu.SemaphoreType.DMA((2,)),
        ],
        compiler_params=params,
        cost_estimate=pl.CostEstimate(flops=2000000, bytes_accessed=1000000, transcendentals=0),
        name="write_returns",
    )(sums, reach, carries, afters, stats, kept_own, *others)
    advantages = pl.pallas_call(
        functools.partial(scale_kernel, float(moves_all * rows * groups)),
        out_shape=block,
        in_specs=[VMEM] * (2 + len(received)),
        out_specs=HBM,
        scratch_shapes=[
            pltpu.VMEM((rows, moves), jnp.float32),
            pltpu.VMEM((rows, LANES), jnp.float32),
            pltpu.SemaphoreType.DMA((1,)),
        ],
        compiler_params=params,
        name="scale",
    )(raw, squares, *received)
    return returns, advantages, loss


def solution(mesh):
    return jax.shard_map(
        per_device,
        mesh=mesh,
        in_specs=(
            P("games", "tm"),
            P("games", "tm"),
            P("member", "games", "tm"),
            P("games"),
            P("games"),
        ),
        out_specs=(P("games", "tm"), P("games", "tm"), P("member", "games")),
        check_vma=False,
    )
```

```python
import functools

import jax
import jax.numpy as jnp
from jax import lax
from jax.experimental import pallas as pl
from jax.experimental.pallas import tpu as pltpu
from jax.sharding import PartitionSpec as P

LANES = 128
SUBLANES = 8
CHUNK = LANES // SUBLANES
PITCH = CHUNK + 1
DEPTH = SUBLANES * PITCH
SLOT = 16
GUESSES = 3
SUMS = 8
LOSSES = SUMS + 3
VMEM = pl.BlockSpec(memory_space=pltpu.VMEM)
HBM = pl.BlockSpec(memory_space=pltpu.HBM)
VMEM_LIMIT = 4 << 20


def iotas(rows):
    shape = (rows, LANES)
    return (
        lax.broadcasted_iota(jnp.int32, shape, 0),
        lax.broadcasted_iota(jnp.int32, shape, 1),
    )


def spread(column, rows):
    return jnp.broadcast_to(column, (rows, LANES))


def at(j):
    return slice(j * LANES, (j + 1) * LANES)


def turn(ref, block, tiles):
    flat = jnp.concatenate(tiles, axis=0).T
    for s in range(SUBLANES):
        start = block * DEPTH + s * PITCH
        ref[start : start + CHUNK, :] = flat[s * CHUNK : (s + 1) * CHUNK]


def chunk_rows(ref, block):
    starts = [block * DEPTH + s * PITCH for s in range(SUBLANES)]
    return [ref[start : start + CHUNK, :] for start in starts]


def strip(block, v):
    return pl.ds(block * DEPTH + v, SUBLANES, stride=PITCH)


def from_next(moved, edge, fill):
    following = moved[1:] + [fill]
    return [jnp.where(edge, far, near) for near, far in zip(moved, following)]


def next_chunk(blocks, rows, fill):
    sub, lane = iotas(SUBLANES)
    up = [pltpu.roll(x, SUBLANES - 1, 0) for x in blocks]
    across = from_next([pltpu.roll(x, LANES - rows, 1) for x in up], lane >= LANES - rows, fill)
    return [jnp.where(sub == SUBLANES - 1, far, near) for near, far in zip(up, across)]


def tree_sum(terms):
    while len(terms) > 1:
        odd = terms[-1:] if len(terms) % 2 else []
        terms = [x + y for x, y in zip(terms[::2], terms[1::2])] + odd
    return terms[0]


def product(terms):
    while len(terms) > 1:
        odd = terms[-1:] if len(terms) % 2 else []
        terms = [x * y for x, y in zip(terms[::2], terms[1::2])] + odd
    return terms[0]


def chunks_on(x):
    return [pltpu.roll(x, SUBLANES - k, 0) for k in range(1, SUBLANES)]


def tiles_on(x, rows):
    return [pltpu.roll(x, LANES - k * rows, 1) for k in range(1, LANES // rows)]


def spans(x, onward, place, count):
    one = jnp.ones_like(x)
    run, wrapped = one, one
    between, parts = [], []
    for k in range(1, count):
        inside = place + k < count
        value = onward[k - 1]
        between.append(jnp.where(inside, run, 0.0))
        parts.append((inside, run, wrapped))
        run = run * jnp.where(inside, value, 1.0)
        wrapped = wrapped * jnp.where(inside, 1.0, value)
    here = x * wrapped
    before = [wrapped] + [jnp.where(inside, here * ran, gone) for inside, ran, gone in parts]
    return between, run, here * run, before


def per_row(column, rows):
    sub, lane = iotas(rows)
    picked = jnp.where(lax.rem(lane, rows) == sub, column, 0.0)
    return jnp.broadcast_to(jnp.sum(picked, axis=0, keepdims=True), (SUBLANES, LANES))


def decay_kernel(
    rewards, dones, own, discount, trace,
    own_out, rewards_turned, own_turned, decay_out, reach_out,
    powers_out, consts_out,
    rewards_in, dones_in, discount_in, trace_in, work, sems,
):
    rows, moves = dones_in.shape
    group = LANES // rows
    count = moves // (LANES * group)
    sub, lane = iotas(SUBLANES)
    pairs = (
        (discount, discount_in),
        (trace, trace_in),
        (dones, dones_in),
        (own, own_out),
        (rewards, rewards_in),
    )
    copies = [pltpu.make_async_copy(*pair, sems.at[k]) for k, pair in enumerate(pairs)]
    for copy in copies:
        copy.start()

    def across(row):
        row = jnp.pad(row, ((0, 0), (0, LANES - rows)))
        row = jnp.broadcast_to(row, (SUBLANES, LANES))
        return tree_sum([row] + tiles_on(row, rows))

    copies[0].wait()
    copies[1].wait()
    disc, lam = across(discount_in[...]), across(trace_in[...])
    rate = disc * lam
    consts_out[0] = rate
    consts_out[1] = (1.0 - lam) / lam
    for copy in copies[2:]:
        copy.wait()
    for b in range(count):
        tiles = [dones_in[:, at(b * group + t)].astype(jnp.float32) for t in range(group)]
        turn(work, b, tiles)
    powers = []
    for b in range(count):
        reach, power = None, jnp.zeros((SUBLANES, LANES), jnp.float32)
        for v in reversed(range(CHUNK)):
            a = rate * (1.0 - work[strip(b, v), :])
            reach = a if reach is None else a * reach
            decay_out[b, v] = a
            reach_out[b, v] = reach
            power += reach * reach
        powers.append(power)
    for b in range(count):
        powers_out[b] = powers[b]
    for k, ref in ((2, rewards_in), (3, own_out)):
        consts_out[k] = per_row(spread(ref[:, moves - 1 : moves], rows), rows)
    for src, dst in ((own_out, own_turned), (rewards_in, rewards_turned)):
        for b in range(count):
            turn(dst, b, [src[:, at(b * group + t)] for t in range(group)])


def local_kernel(rewards, own, *refs):
    members = lax.axis_size("member")
    others, refs = refs[: members - 1], refs[members - 1 :]
    decay, reach, powers, consts, sums, carry_out, after_out, stats_out, folds, *works = refs
    rows, moves = others[0].shape
    group = LANES // rows
    count = moves // (LANES * group)
    sub, lane = iotas(SUBLANES)
    block, blocks = lax.axis_index("tm"), lax.axis_size("tm")
    me = lax.axis_index("member")
    first = (place_of(LANES // (blocks * SLOT)) * blocks + block) * SLOT
    rate, ratio, last_reward, last_own = (consts[k] for k in range(4))
    values = [own, *works]
    for b in range(count):
        for src, dst in zip(others, works):
            turn(dst, b, [src[:, at(b * group + t)] for t in range(group)])

    chunk_gates, tile_gates = [], []
    insides, lasts, wholes, afters = [], [], [], [None] * count
    for b in range(count):
        total = reach[b, 0]
        between, inside, whole, before = spans(total, chunks_on(total), sub, SUBLANES)
        chunk_gates.append((between, before))
        insides.append(inside)
        between, last, whole, before = spans(whole, tiles_on(whole, rows), lane // rows, group)
        tile_gates.append((between, before))
        lasts.append(last)
        wholes.append(whole)
    beyond = jnp.ones((SUBLANES, LANES), jnp.float32)
    squares = jnp.zeros((SUBLANES, LANES), jnp.float32)
    for b in reversed(range(count)):
        afters[b] = insides[b] * lasts[b] * beyond
        after_out[b] = afters[b]
        beyond = beyond * wholes[b]
        squares += powers[b] * (afters[b] * afters[b])
    slope = reach[0, 0] * afters[0]

    def mean_of(parts):
        return sum(parts[1:], parts[0]) / members

    def guess_of(value):
        return jnp.where(block == blocks - 1, 0.0, (value - last_reward) / rate)

    ends = [last_own]
    ends += [per_row(spread(ref[:, moves - 1 : moves], rows), rows) for ref in others]
    guess = guess_of(mean_of(ends))
    guesses = [guess_of(end) for end in ends]

    zero = jnp.zeros((SUBLANES, LANES), jnp.float32)

    def mean_at(b, v):
        return mean_of([ref[strip(b, v), :] for ref in values])

    followers = next_chunk([mean_at(b, 0) for b in range(count)], rows, zero)
    withins, tiles = [], []
    for b in range(count):
        following, total = followers[b], None
        for v in reversed(range(CHUNK)):
            a = decay[b, v]
            x = rewards[strip(b, v), :] + ratio * a * following
            following = mean_at(b, v)
            total = x if total is None else x + a * total
            sums[b, v] = total
        moved = chunks_on(total)
        between, before = chunk_gates[b]
        withins.append(tree_sum([gate * x for gate, x in zip(between, moved)]))
        tiles.append(tree_sum([gate * x for gate, x in zip(before, [total] + moved)]))
    beyond = zero
    carries = [None] * count
    for b in reversed(range(count)):
        moved = tiles_on(tiles[b], rows)
        between, before = tile_gates[b]
        onward = tree_sum([gate * x for gate, x in zip(between, moved)]) + lasts[b] * beyond
        carries[b] = withins[b] + insides[b] * onward + afters[b] * guess
        if b:
            whole = tree_sum([gate * x for gate, x in zip(before, [tiles[b]] + moved)])
            beyond = whole + wholes[b] * beyond

    head = sums[0, 0] + reach[0, 0] * carries[0] + ratio * mean_at(0, 0)
    total = zero
    sqq, sqa = [zero] * members, [zero] * members
    for b in range(count):
        carry, after = carries[b], afters[b]
        carry_out[b] = carry
        own_carries = [carry + after * (own_guess - guess) for own_guess in guesses]
        part_qa = [zero] * members
        for v in range(CHUNK):
            weight, partial = reach[b, v], sums[b, v]
            error = None
            for m, ref in enumerate(values):
                q = ref[strip(b, v), :] - partial - weight * own_carries[m]
                sqq[m] += q * q
                part_qa[m] += q * weight
                error = q if error is None else error + q
            total += error * error
        for m in range(members):
            sqa[m] += part_qa[m] * after
    suu = total / (members * members)
    sua = -sum(sqa[1:], sqa[0]) / members

    def by_member(entries, m):
        found = entries[0]
        for turn_of in range(1, members):
            found = jnp.where(lax.rem(me + turn_of, members) == m, entries[turn_of], found)
        return found

    held = jnp.where(sub == 0, head, zero)
    singles = [slope, guess] + [by_member(guesses, m) for m in range(members)]
    for k, entry in enumerate(singles):
        held = jnp.where(sub == 1 + k, jnp.broadcast_to(entry[:1], held.shape), held)
    held = jnp.where(lane < rows, held, 0.0)
    totals = [suu, sua, squares]
    for m in range(members):
        totals += [by_member(sqq, m), by_member(sqa, m)]
    totals += [zero] * (SUBLANES - len(totals))
    for k, entry in enumerate(totals):
        folds[k * (SUBLANES + 1) : k * (SUBLANES + 1) + SUBLANES, :] = entry
    folded = tree_sum(
        [folds[pl.ds(s, SUBLANES, stride=SUBLANES + 1), :] for s in range(SUBLANES)]
    )
    flat = jnp.concatenate([held, folded], axis=0).T
    per_game = tree_sum([flat[t * rows : (t + 1) * rows] for t in range(group)])
    padded = jnp.pad(per_game, ((0, 0), (0, LANES - SLOT)))
    stats_out[...] = pltpu.roll(padded, first, 1)


def chain(stats, blocks, picks):
    ahead = jnp.zeros_like(stats)
    for t in reversed(range(blocks)):
        moved = {k: pltpu.roll(stats, (LANES - t * SLOT - k) % LANES, 1) for k in picks}
        eps = ahead - moved[2]
        yield t, ahead, eps, moved
        ahead = moved[0] + moved[1] * eps


def squares_of(stats, blocks):
    sub, lane = iotas(stats.shape[0])
    found = jnp.zeros_like(stats)
    for t, ahead, eps, moved in chain(stats, blocks, (0, 1, 2, SUMS, SUMS + 1, SUMS + 2)):
        suu, sua, saa = (moved[SUMS + k] for k in range(3))
        found += suu + eps * (2.0 * sua + eps * saa)
    return jnp.where(lax.rem(lane, blocks * SLOT) == 0, found, 0.0)


def returns_kernel(
    moves_all, sums, reach, carries, afters, stats, *refs
):
    members = lax.axis_size("member")
    values, refs = refs[:members], refs[members:]
    returns_out, loss_out, raw_out, squares_out, returns, loss, work, sems = refs
    rows, moves = values[0].shape
    group = LANES // rows
    count = moves // (LANES * group)
    sub, lane = iotas(rows)
    blocks = lax.axis_size("tm")
    block, me = lax.axis_index("tm"), lax.axis_index("member")
    first = place_of(LANES // (blocks * SLOT)) * blocks * SLOT
    zero = jnp.zeros((rows, LANES), jnp.float32)
    own_eps, own_loss = zero, zero
    squares_out[...] = squares_of(stats[...], blocks)
    for t, ahead, eps, moved in chain(stats[...], blocks, range(LOSSES + 2 * members)):
        saa = moved[SUMS + 2]
        own_eps += jnp.where((lane == first) & (block == t), eps, 0.0)
        for m in range(members):
            sqq, sqa = moved[LOSSES + 2 * m], moved[LOSSES + 2 * m + 1]
            guess = moved[GUESSES + m]
            off = ahead - guess
            term = sqq + off * (off * saa - 2.0 * sqa)
            own_loss += jnp.where((lane == first) & (me == m), term, 0.0)
    eps = spread(jnp.sum(own_eps, axis=1, keepdims=True), rows)
    eps = per_row(eps, rows)
    for b in range(count):
        carry = carries[b] + afters[b] * eps
        for v in range(CHUNK):
            work[strip(b, v), :] = sums[b, v] + reach[b, v] * carry
        flat = jnp.concatenate(chunk_rows(work, b), axis=0).T
        for t in range(group):
            j = b * group + t
            result = flat[t * rows : (t + 1) * rows]
            returns[:, at(j)] = result
            parts = [ref[:, at(j)] for ref in values]
            raw_out[:, at(j)] = result - sum(parts[1:], parts[0]) / members
    column = spread(jnp.sum(own_loss, axis=1, keepdims=True), rows)
    loss_row = jnp.sum(jnp.where(lane == sub, column, 0.0), axis=0, keepdims=True)
    loss[...] = loss_row[:, :rows] / moves_all
    copies = [
        pltpu.make_async_copy(returns, returns_out, sems.at[0]),
        pltpu.make_async_copy(loss, loss_out, sems.at[1]),
    ]
    for copy in copies:
        copy.start()
    for copy in copies:
        copy.wait()


def scale_kernel(cells_all, raw, squares, *refs):
    *stats, adv_out, adv, rows_in, sems = refs
    rows, moves = raw.shape
    tiles = moves // LANES
    found = squares[...]
    for ref in stats:
        for n in range(ref.shape[0]):
            found += squares_of(ref[n], lax.axis_size("tm"))
    rows_in[...] = found
    found = tree_sum([jnp.broadcast_to(rows_in[s : s + 1, :], found.shape) for s in range(rows)])
    total = spread(jnp.sum(found, axis=1, keepdims=True), rows)
    norm_scale = lax.rsqrt(total / cells_all + 1e-06)
    for j in range(tiles):
        adv[:, at(j)] = raw[:, at(j)] * norm_scale
    copy = pltpu.make_async_copy(adv, adv_out, sems.at[0])
    copy.start()
    copy.wait()


def exchange(value, axis, bit):
    names = ("tm", "games", "member")
    sizes = [lax.axis_size(name) for name in names]
    pairs = []
    for t in range(sizes[0]):
        for g in range(sizes[1]):
            for m in range(sizes[2]):
                to = [t, g, (m + 1) % sizes[2]]
                to[names.index(axis)] ^= bit
                pairs.append(
                    ((t * sizes[1] + g) * sizes[2] + m, (to[0] * sizes[1] + to[1]) * sizes[2] + to[2])
                )
    return lax.ppermute(value, names, pairs)


def bits(count):
    return [1 << k for k in reversed(range(count.bit_length() - 1))]


def place_of(packed):
    groups = lax.axis_size("games")
    return lax.axis_index("games") // max(1, groups // packed)


def per_device(rewards, dones, values, discount, trace):
    members = lax.axis_size("member")
    blocks = lax.axis_size("tm")
    groups = lax.axis_size("games")
    own = values[0]
    rows, moves = own.shape
    others = [
        lax.ppermute(own, "member", [(m, (m + turn) % members) for m in range(members)])
        for turn in range(members - 1, 0, -1)
    ]

    def array(*shape):
        return jax.ShapeDtypeStruct(shape, jnp.float32)

    params = pltpu.CompilerParams(vmem_limit_bytes=VMEM_LIMIT)
    block = array(rows, moves)
    group = LANES // rows
    count = moves // (LANES * group)
    flat = array(count * DEPTH, LANES)
    strips = array(count, CHUNK, SUBLANES, LANES)
    row = pltpu.VMEM((1, rows), jnp.float32)
    kept_own, *kept = pl.pallas_call(
        decay_kernel,
        out_shape=(
            block, flat, flat, strips, strips,
            array(count, SUBLANES, LANES),
            array(4, SUBLANES, LANES),
        ),
        in_specs=[HBM] * 5,
        out_specs=(VMEM,) * 7,
        scratch_shapes=[
            pltpu.VMEM((rows, moves), jnp.float32),
            pltpu.VMEM((rows, moves), jnp.int32),
            row,
            row,
            pltpu.VMEM((count * DEPTH, LANES), jnp.float32),
            pltpu.SemaphoreType.DMA((5,)),
        ],
        compiler_params=params,
        cost_estimate=pl.CostEstimate(flops=4000000, bytes_accessed=2000000, transcendentals=0),
        name="decay_scan",
    )(
        *(
            pltpu.with_memory_space_constraint(x, pltpu.HBM)
            for x in (rewards, dones, own, discount[None], trace[None])
        )
    )
    rewards_turned, own_turned, decay, reach, powers, consts = kept
    sums, carries, afters, stats = pl.pallas_call(
        local_kernel,
        out_shape=(strips, *[array(count, SUBLANES, LANES)] * 2, array(rows, LANES)),
        in_specs=[VMEM] * (members + 5),
        out_specs=(VMEM,) * 4,
        scratch_shapes=[
            pltpu.VMEM((SUBLANES * (SUBLANES + 1), LANES), jnp.float32),
        ]
        + [pltpu.VMEM((count * DEPTH, LANES), jnp.float32)] * (members - 1),
        compiler_params=params,
        name="local_scan",
    )(rewards_turned, own_turned, *others, decay, reach, powers, consts)

    stats = sum((exchange(stats, "tm", mask) for mask in range(1, blocks)), stats)
    packed = LANES // (blocks * SLOT)
    for bit in bits(groups)[: len(bits(packed))]:
        stats = stats + exchange(stats, "games", bit)
    held, received = stats[None], []
    for bit in bits(groups)[len(bits(packed)) :]:
        if received:
            held = jnp.concatenate([held, received[-1]])
        received.append(exchange(held, "games", bit))
    moves_all = moves * blocks
    returns, loss, raw, squares = pl.pallas_call(
        functools.partial(returns_kernel, float(moves_all)),
        out_shape=(block, array(1, rows), block, array(rows, LANES)),
        in_specs=[VMEM] * (5 + members),
        out_specs=(HBM, HBM, VMEM, VMEM),
        scratch_shapes=[
            pltpu.VMEM((rows, moves), jnp.float32),
            pltpu.VMEM((1, rows), jnp.float32),
            pltpu.VMEM((count * DEPTH, LANES), jnp.float32),
            pltpu.SemaphoreType.DMA((2,)),
        ],
        compiler_params=params,
        cost_estimate=pl.CostEstimate(flops=2000000, bytes_accessed=1000000, transcendentals=0),
        name="write_returns",
    )(sums, reach, carries, afters, stats, kept_own, *others)
    advantages = pl.pallas_call(
        functools.partial(scale_kernel, float(moves_all * rows * groups)),
        out_shape=block,
        in_specs=[VMEM] * (2 + len(received)),
        out_specs=HBM,
        scratch_shapes=[
            pltpu.VMEM((rows, moves), jnp.float32),
            pltpu.VMEM((rows, LANES), jnp.float32),
            pltpu.SemaphoreType.DMA((1,)),
        ],
        compiler_params=params,
        name="scale",
    )(raw, squares, *received)
    return returns, advantages, loss


def solution(mesh):
    return jax.shard_map(
        per_device,
        mesh=mesh,
        in_specs=(
            P("games", "tm"),
            P("games", "tm"),
            P("member", "games", "tm"),
            P("games"),
            P("games"),
        ),
        out_specs=(P("games", "tm"), P("games", "tm"), P("member", "games")),
        check_vma=False,
    )
```

```python
import functools

import jax
import jax.numpy as jnp
from jax import lax
from jax.experimental import pallas as pl
from jax.experimental.pallas import tpu as pltpu
from jax.sharding import PartitionSpec as P

LANES = 128
SUBLANES = 8
CHUNK = LANES // SUBLANES
PITCH = CHUNK + 1
DEPTH = SUBLANES * PITCH
SLOT = 16
GUESSES = 3
SUMS = 8
LOSSES = SUMS + 3
VMEM = pl.BlockSpec(memory_space=pltpu.VMEM)
HBM = pl.BlockSpec(memory_space=pltpu.HBM)
VMEM_LIMIT = 4 << 20


def iotas(rows):
    shape = (rows, LANES)
    return (
        lax.broadcasted_iota(jnp.int32, shape, 0),
        lax.broadcasted_iota(jnp.int32, shape, 1),
    )


def spread(column, rows):
    return jnp.broadcast_to(column, (rows, LANES))


def at(j):
    return slice(j * LANES, (j + 1) * LANES)


def turn(ref, block, tiles):
    flat = jnp.concatenate(tiles, axis=0).T
    for s in range(SUBLANES):
        start = block * DEPTH + s * PITCH
        ref[start : start + CHUNK, :] = flat[s * CHUNK : (s + 1) * CHUNK]


def chunk_rows(ref, block):
    starts = [block * DEPTH + s * PITCH for s in range(SUBLANES)]
    return [ref[start : start + CHUNK, :] for start in starts]


def strip(block, v):
    return pl.ds(block * DEPTH + v, SUBLANES, stride=PITCH)


def from_next(moved, edge, fill):
    following = moved[1:] + [fill]
    return [jnp.where(edge, far, near) for near, far in zip(moved, following)]


def next_chunk(blocks, rows, fill):
    sub, lane = iotas(SUBLANES)
    up = [pltpu.roll(x, SUBLANES - 1, 0) for x in blocks]
    across = from_next([pltpu.roll(x, LANES - rows, 1) for x in up], lane >= LANES - rows, fill)
    return [jnp.where(sub == SUBLANES - 1, far, near) for near, far in zip(up, across)]


def tree_sum(terms):
    while len(terms) > 1:
        odd = terms[-1:] if len(terms) % 2 else []
        terms = [x + y for x, y in zip(terms[::2], terms[1::2])] + odd
    return terms[0]


def product(terms):
    while len(terms) > 1:
        odd = terms[-1:] if len(terms) % 2 else []
        terms = [x * y for x, y in zip(terms[::2], terms[1::2])] + odd
    return terms[0]


def chunks_on(x):
    return [pltpu.roll(x, SUBLANES - k, 0) for k in range(1, SUBLANES)]


def tiles_on(x, rows):
    return [pltpu.roll(x, LANES - k * rows, 1) for k in range(1, LANES // rows)]


def spans(x, onward, place, count):
    one = jnp.ones_like(x)
    run, wrapped = one, one
    between, parts = [], []
    for k in range(1, count):
        inside = place + k < count
        value = onward[k - 1]
        between.append(jnp.where(inside, run, 0.0))
        parts.append((inside, run, wrapped))
        run = run * jnp.where(inside, value, 1.0)
        wrapped = wrapped * jnp.where(inside, 1.0, value)
    here = x * wrapped
    before = [wrapped] + [jnp.where(inside, here * ran, gone) for inside, ran, gone in parts]
    return between, run, here * run, before


def per_row(column, rows):
    sub, lane = iotas(rows)
    picked = jnp.where(lax.rem(lane, rows) == sub, column, 0.0)
    return jnp.broadcast_to(jnp.sum(picked, axis=0, keepdims=True), (SUBLANES, LANES))


def decay_kernel(
    rewards, dones, own, discount, trace,
    own_out, rewards_turned, own_turned, decay_out, consts_out,
    rewards_in, dones_in, discount_in, trace_in, work, sems,
):
    rows, moves = dones_in.shape
    group = LANES // rows
    count = moves // (LANES * group)
    sub, lane = iotas(SUBLANES)
    pairs = (
        (discount, discount_in),
        (trace, trace_in),
        (dones, dones_in),
        (own, own_out),
        (rewards, rewards_in),
    )
    copies = [pltpu.make_async_copy(*pair, sems.at[k]) for k, pair in enumerate(pairs)]
    for copy in copies:
        copy.start()

    def across(row):
        row = jnp.pad(row, ((0, 0), (0, LANES - rows)))
        row = jnp.broadcast_to(row, (SUBLANES, LANES))
        return tree_sum([row] + tiles_on(row, rows))

    copies[0].wait()
    copies[1].wait()
    disc, lam = across(discount_in[...]), across(trace_in[...])
    rate = disc * lam
    consts_out[0] = rate
    consts_out[1] = (1.0 - lam) / lam
    for copy in copies[2:]:
        copy.wait()
    for b in range(count):
        tiles = [dones_in[:, at(b * group + t)].astype(jnp.float32) for t in range(group)]
        turn(work, b, tiles)
    for b in range(count):
        for v in range(CHUNK):
            decay_out[b, v] = rate * (1.0 - work[strip(b, v), :])
    for k, ref in ((2, rewards_in), (3, own_out)):
        consts_out[k] = per_row(spread(ref[:, moves - 1 : moves], rows), rows)
    for src, dst in ((own_out, own_turned), (rewards_in, rewards_turned)):
        for b in range(count):
            turn(dst, b, [src[:, at(b * group + t)] for t in range(group)])


def local_kernel(rewards, own, *refs):
    members = lax.axis_size("member")
    others, refs = refs[: members - 1], refs[members - 1 :]
    decay, consts, sums, reach, carry_out, after_out, stats_out, folds, *works = refs
    rows, moves = others[0].shape
    group = LANES // rows
    count = moves // (LANES * group)
    sub, lane = iotas(SUBLANES)
    block, blocks = lax.axis_index("tm"), lax.axis_size("tm")
    me = lax.axis_index("member")
    first = (lax.rem(lax.axis_index("games"), LANES // (blocks * SLOT)) * blocks + block) * SLOT
    rate, ratio, last_reward, last_own = (consts[k] for k in range(4))
    values = [own, *works]
    for b in range(count):
        for src, dst in zip(others, works):
            turn(dst, b, [src[:, at(b * group + t)] for t in range(group)])

    chunk_gates, tile_gates = [], []
    insides, lasts, wholes, powers, afters = [], [], [], [], [None] * count
    for b in range(count):
        total, power = None, jnp.zeros((SUBLANES, LANES), jnp.float32)
        for v in reversed(range(CHUNK)):
            total = decay[b, v] if total is None else decay[b, v] * total
            reach[b, v] = total
            power += total * total
        powers.append(power)
        between, inside, whole, before = spans(total, chunks_on(total), sub, SUBLANES)
        chunk_gates.append((between, before))
        insides.append(inside)
        between, last, whole, before = spans(whole, tiles_on(whole, rows), lane // rows, group)
        tile_gates.append((between, before))
        lasts.append(last)
        wholes.append(whole)
    beyond = jnp.ones((SUBLANES, LANES), jnp.float32)
    squares = jnp.zeros((SUBLANES, LANES), jnp.float32)
    for b in reversed(range(count)):
        afters[b] = insides[b] * lasts[b] * beyond
        after_out[b] = afters[b]
        beyond = beyond * wholes[b]
        squares += powers[b] * (afters[b] * afters[b])
    slope = reach[0, 0] * afters[0]

    def mean_of(parts):
        return sum(parts[1:], parts[0]) / members

    def guess_of(value):
        return jnp.where(block == blocks - 1, 0.0, (value - last_reward) / rate)

    ends = [last_own]
    ends += [per_row(spread(ref[:, moves - 1 : moves], rows), rows) for ref in others]
    guess = guess_of(mean_of(ends))
    guesses = [guess_of(end) for end in ends]

    zero = jnp.zeros((SUBLANES, LANES), jnp.float32)

    def mean_at(b, v):
        return mean_of([ref[strip(b, v), :] for ref in values])

    followers = next_chunk([mean_at(b, 0) for b in range(count)], rows, zero)
    withins, tiles = [], []
    for b in range(count):
        following, total = followers[b], None
        for v in reversed(range(CHUNK)):
            a = decay[b, v]
            x = rewards[strip(b, v), :] + ratio * a * following
            following = mean_at(b, v)
            total = x if total is None else x + a * total
            sums[b, v] = total
        moved = chunks_on(total)
        between, before = chunk_gates[b]
        withins.append(tree_sum([gate * x for gate, x in zip(between, moved)]))
        tiles.append(tree_sum([gate * x for gate, x in zip(before, [total] + moved)]))
    beyond = zero
    carries = [None] * count
    for b in reversed(range(count)):
        moved = tiles_on(tiles[b], rows)
        between, before = tile_gates[b]
        onward = tree_sum([gate * x for gate, x in zip(between, moved)]) + lasts[b] * beyond
        carries[b] = withins[b] + insides[b] * onward + afters[b] * guess
        if b:
            whole = tree_sum([gate * x for gate, x in zip(before, [tiles[b]] + moved)])
            beyond = whole + wholes[b] * beyond

    head = sums[0, 0] + reach[0, 0] * carries[0] + ratio * mean_at(0, 0)
    total = zero
    sqq, sqa = [zero] * members, [zero] * members
    for b in range(count):
        carry, after = carries[b], afters[b]
        carry_out[b] = carry
        own_carries = [carry + after * (own_guess - guess) for own_guess in guesses]
        part_qa = [zero] * members
        for v in range(CHUNK):
            weight, partial = reach[b, v], sums[b, v]
            error = None
            for m, ref in enumerate(values):
                q = ref[strip(b, v), :] - partial - weight * own_carries[m]
                sqq[m] += q * q
                part_qa[m] += q * weight
                error = q if error is None else error + q
            total += error * error
        for m in range(members):
            sqa[m] += part_qa[m] * after
    suu = total / (members * members)
    sua = -sum(sqa[1:], sqa[0]) / members

    def by_member(entries, m):
        found = entries[0]
        for turn_of in range(1, members):
            found = jnp.where(lax.rem(me + turn_of, members) == m, entries[turn_of], found)
        return found

    held = jnp.where(sub == 0, head, zero)
    singles = [slope, guess] + [by_member(guesses, m) for m in range(members)]
    for k, entry in enumerate(singles):
        held = jnp.where(sub == 1 + k, jnp.broadcast_to(entry[:1], held.shape), held)
    held = jnp.where(lane < rows, held, 0.0)
    totals = [suu, sua, squares]
    for m in range(members):
        totals += [by_member(sqq, m), by_member(sqa, m)]
    totals += [zero] * (SUBLANES - len(totals))
    for k, entry in enumerate(totals):
        folds[k * (SUBLANES + 1) : k * (SUBLANES + 1) + SUBLANES, :] = entry
    folded = tree_sum(
        [folds[pl.ds(s, SUBLANES, stride=SUBLANES + 1), :] for s in range(SUBLANES)]
    )
    flat = jnp.concatenate([held, folded], axis=0).T
    per_game = tree_sum([flat[t * rows : (t + 1) * rows] for t in range(group)])
    padded = jnp.pad(per_game, ((0, 0), (0, LANES - SLOT)))
    stats_out[...] = pltpu.roll(padded, first, 1)


def chain(stats, blocks, picks):
    ahead = jnp.zeros_like(stats)
    for t in reversed(range(blocks)):
        moved = {k: pltpu.roll(stats, (LANES - t * SLOT - k) % LANES, 1) for k in picks}
        eps = ahead - moved[2]
        yield t, ahead, eps, moved
        ahead = moved[0] + moved[1] * eps


def squares_of(stats, blocks):
    sub, lane = iotas(stats.shape[0])
    found = jnp.zeros_like(stats)
    for t, ahead, eps, moved in chain(stats, blocks, (0, 1, 2, SUMS, SUMS + 1, SUMS + 2)):
        suu, sua, saa = (moved[SUMS + k] for k in range(3))
        found += suu + eps * (2.0 * sua + eps * saa)
    return jnp.where(lax.rem(lane, blocks * SLOT) == 0, found, 0.0)


def returns_kernel(
    moves_all, sums, reach, carries, afters, stats, *refs
):
    members = lax.axis_size("member")
    values, refs = refs[:members], refs[members:]
    returns_out, loss_out, raw_out, squares_out, returns, loss, work, sems = refs
    rows, moves = values[0].shape
    group = LANES // rows
    count = moves // (LANES * group)
    sub, lane = iotas(rows)
    blocks = lax.axis_size("tm")
    block, me = lax.axis_index("tm"), lax.axis_index("member")
    first = lax.rem(lax.axis_index("games"), LANES // (blocks * SLOT)) * blocks * SLOT
    zero = jnp.zeros((rows, LANES), jnp.float32)
    own_eps, own_loss = zero, zero
    squares_out[...] = squares_of(stats[...], blocks)
    for t, ahead, eps, moved in chain(stats[...], blocks, range(LOSSES + 2 * members)):
        saa = moved[SUMS + 2]
        own_eps += jnp.where((lane == first) & (block == t), eps, 0.0)
        for m in range(members):
            sqq, sqa = moved[LOSSES + 2 * m], moved[LOSSES + 2 * m + 1]
            guess = moved[GUESSES + m]
            off = ahead - guess
            term = sqq + off * (off * saa - 2.0 * sqa)
            own_loss += jnp.where((lane == first) & (me == m), term, 0.0)
    eps = spread(jnp.sum(own_eps, axis=1, keepdims=True), rows)
    eps = per_row(eps, rows)
    for b in range(count):
        carry = carries[b] + afters[b] * eps
        for v in range(CHUNK):
            work[strip(b, v), :] = sums[b, v] + reach[b, v] * carry
        flat = jnp.concatenate(chunk_rows(work, b), axis=0).T
        for t in range(group):
            j = b * group + t
            result = flat[t * rows : (t + 1) * rows]
            returns[:, at(j)] = result
            parts = [ref[:, at(j)] for ref in values]
            raw_out[:, at(j)] = result - sum(parts[1:], parts[0]) / members
    column = spread(jnp.sum(own_loss, axis=1, keepdims=True), rows)
    loss_row = jnp.sum(jnp.where(lane == sub, column, 0.0), axis=0, keepdims=True)
    loss[...] = loss_row[:, :rows] / moves_all
    copies = [
        pltpu.make_async_copy(returns, returns_out, sems.at[0]),
        pltpu.make_async_copy(loss, loss_out, sems.at[1]),
    ]
    for copy in copies:
        copy.start()
    for copy in copies:
        copy.wait()


def scale_kernel(cells_all, raw, squares, *refs):
    *stats, adv_out, adv, rows_in, sems = refs
    rows, moves = raw.shape
    tiles = moves // LANES
    found = squares[...]
    for ref in stats:
        for n in range(ref.shape[0]):
            found += squares_of(ref[n], lax.axis_size("tm"))
    rows_in[...] = found
    found = tree_sum([jnp.broadcast_to(rows_in[s : s + 1, :], found.shape) for s in range(rows)])
    total = spread(jnp.sum(found, axis=1, keepdims=True), rows)
    norm_scale = lax.rsqrt(total / cells_all + 1e-06)
    for j in range(tiles):
        adv[:, at(j)] = raw[:, at(j)] * norm_scale
    copy = pltpu.make_async_copy(adv, adv_out, sems.at[0])
    copy.start()
    copy.wait()


def exchange(value, axis, bit):
    names = ("tm", "games", "member")
    sizes = [lax.axis_size(name) for name in names]
    pairs = []
    for t in range(sizes[0]):
        for g in range(sizes[1]):
            for m in range(sizes[2]):
                to = [t, g, (m + 1) % sizes[2]]
                to[names.index(axis)] ^= bit
                pairs.append(
                    ((t * sizes[1] + g) * sizes[2] + m, (to[0] * sizes[1] + to[1]) * sizes[2] + to[2])
                )
    return lax.ppermute(value, names, pairs)


def bits(count):
    return [1 << k for k in range(count.bit_length() - 1)]


def per_device(rewards, dones, values, discount, trace):
    members = lax.axis_size("member")
    blocks = lax.axis_size("tm")
    groups = lax.axis_size("games")
    own = values[0]
    rows, moves = own.shape
    others = [
        lax.ppermute(own, "member", [(m, (m + turn) % members) for m in range(members)])
        for turn in range(members - 1, 0, -1)
    ]

    def array(*shape):
        return jax.ShapeDtypeStruct(shape, jnp.float32)

    params = pltpu.CompilerParams(vmem_limit_bytes=VMEM_LIMIT)
    block = array(rows, moves)
    group = LANES // rows
    count = moves // (LANES * group)
    flat = array(count * DEPTH, LANES)
    strips = array(count, CHUNK, SUBLANES, LANES)
    row = pltpu.VMEM((1, rows), jnp.float32)
    kept_own, *kept = pl.pallas_call(
        decay_kernel,
        out_shape=(
            block, flat, flat, strips,
            array(4, SUBLANES, LANES),
        ),
        in_specs=[HBM] * 5,
        out_specs=(VMEM,) * 5,
        scratch_shapes=[
            pltpu.VMEM((rows, moves), jnp.float32),
            pltpu.VMEM((rows, moves), jnp.int32),
            row,
            row,
            pltpu.VMEM((count * DEPTH, LANES), jnp.float32),
            pltpu.SemaphoreType.DMA((5,)),
        ],
        compiler_params=params,
        cost_estimate=pl.CostEstimate(flops=4000000, bytes_accessed=2000000, transcendentals=0),
        name="decay_scan",
    )(
        *(
            pltpu.with_memory_space_constraint(x, pltpu.HBM)
            for x in (rewards, dones, own, discount[None], trace[None])
        )
    )
    rewards_turned, own_turned, decay, consts = kept
    sums, reach, carries, afters, stats = pl.pallas_call(
        local_kernel,
        out_shape=(strips, strips, *[array(count, SUBLANES, LANES)] * 2, array(rows, LANES)),
        in_specs=[VMEM] * (members + 3),
        out_specs=(VMEM,) * 5,
        scratch_shapes=[
            pltpu.VMEM((SUBLANES * (SUBLANES + 1), LANES), jnp.float32),
        ]
        + [pltpu.VMEM((count * DEPTH, LANES), jnp.float32)] * (members - 1),
        compiler_params=params,
        name="local_scan",
    )(rewards_turned, own_turned, *others, decay, consts)

    stats = sum((exchange(stats, "tm", mask) for mask in range(1, blocks)), stats)
    packed = LANES // (blocks * SLOT)
    for bit in bits(min(groups, packed)):
        stats = stats + exchange(stats, "games", bit)
    held, received = stats[None], []
    for bit in bits(groups)[len(bits(packed)) :]:
        if received:
            held = jnp.concatenate([held, received[-1]])
        received.append(exchange(held, "games", bit))
    moves_all = moves * blocks
    returns, loss, raw, squares = pl.pallas_call(
        functools.partial(returns_kernel, float(moves_all)),
        out_shape=(block, array(1, rows), block, array(rows, LANES)),
        in_specs=[VMEM] * (5 + members),
        out_specs=(HBM, HBM, VMEM, VMEM),
        scratch_shapes=[
            pltpu.VMEM((rows, moves), jnp.float32),
            pltpu.VMEM((1, rows), jnp.float32),
            pltpu.VMEM((count * DEPTH, LANES), jnp.float32),
            pltpu.SemaphoreType.DMA((2,)),
        ],
        compiler_params=params,
        cost_estimate=pl.CostEstimate(flops=2000000, bytes_accessed=1000000, transcendentals=0),
        name="write_returns",
    )(sums, reach, carries, afters, stats, kept_own, *others)
    advantages = pl.pallas_call(
        functools.partial(scale_kernel, float(moves_all * rows * groups)),
        out_shape=block,
        in_specs=[VMEM] * (2 + len(received)),
        out_specs=HBM,
        scratch_shapes=[
            pltpu.VMEM((rows, moves), jnp.float32),
            pltpu.VMEM((rows, LANES), jnp.float32),
            pltpu.SemaphoreType.DMA((1,)),
        ],
        compiler_params=params,
        name="scale",
    )(raw, squares, *received)
    return returns, advantages, loss


def solution(mesh):
    return jax.shard_map(
        per_device,
        mesh=mesh,
        in_specs=(
            P("games", "tm"),
            P("games", "tm"),
            P("member", "games", "tm"),
            P("games"),
            P("games"),
        ),
        out_specs=(P("games", "tm"), P("games", "tm"), P("member", "games")),
        check_vma=False,
    )
```
